256 devices in a mesh: row: 16 (over z_hi, x), col: 16 (over y, z_lo, core).
Axes of the slice: x: 4, y: 4, z: 8 (z_hi: 4, z_lo: 2; z = z_hi * 2 + z_lo), core: 2. Of those that a mesh axis runs over, the one named last changes fastest.
Arguments:
- queries: bfloat16 [16, 768, 768], P('row', 'col'), may hold values from -18 to 18
- keys: bfloat16 [16, 768, 768], P('col', 'row'), may hold values from -18 to 18
Outputs:
- grad_queries: float32 [16, 768, 768], P('row', 'col')
- grad_keys: float32 [16, 768, 768], P('col', 'row')
The draws below stay inside these ranges and needn't reach their ends.
All inputs are finite; a program needn't handle non-finite values.
Results may differ from the reference program's by a relative error of at most 0.005.
Values may be sent and summed in bfloat16 or wider, within the bound.
A program may use at most 64 MiB of HBM per device.

```python
import jax
import jax.numpy as jnp
from jax import lax

D = 768
FRAMES = 16
TOK = 768


def make_view(key, salt):
    base = jax.random.fold_in(key, 7)
    scene_key = jax.random.fold_in(base, 1)
    noise_key = jax.random.fold_in(jax.random.fold_in(base, 11), salt)
    scene = jnp.clip(jax.random.normal(scene_key, (TOK, D), jnp.float32), -4.0, 4.0)
    noise = jnp.clip(jax.random.normal(noise_key, (FRAMES, TOK, D), jnp.float32), -4.0, 4.0)
    view = 0.5 * scene[None] + 0.87 * noise
    return view.astype(jnp.bfloat16)


def draw_queries(key, part):
    return make_view(key, 0)


def draw_keys(key, part):
    return make_view(key, 1)


def setup_inputs(seed: int = 0) -> dict:
    streams_of = jax.random.split(jax.random.key(seed), 3)
    queries = draw_queries(jax.random.fold_in(streams_of[2], 71), 0)
    keys = draw_keys(jax.random.fold_in(streams_of[2], 71), 0)
    return dict(queries=queries, keys=keys)


def contract(left_side, right_side, left_dim, right_dim):
    return lax.dot_general(left_side, right_side, (((left_dim,), (right_dim,)), ((), ())), preferred_element_type=jnp.float32)


def cycle_terms(query_frame, key_frame, score_scale, frames):
    scores = score_scale * contract(query_frame, key_frame, 1, 1)
    by_rows = jax.nn.softmax(scores, axis=1)
    by_cols = jax.nn.softmax(scores, axis=0)
    rows_half = by_rows.astype(jnp.bfloat16)
    cols_half = by_cols.astype(jnp.bfloat16)
    warped = contract(cols_half, query_frame, 0, 0).astype(jnp.bfloat16)
    cycled = jnp.dot(rows_half, warped, preferred_element_type=jnp.float32)
    residual = (cycled - query_frame.astype(jnp.float32)) / frames
    resid_half = residual.astype(jnp.bfloat16)
    grad_rows = contract(resid_half, warped, 1, 1)
    grad_warp = contract(rows_half, resid_half, 0, 0).astype(jnp.bfloat16)
    grad_cols = contract(query_frame, grad_warp, 1, 1)
    grad_scores = by_rows * (grad_rows - jnp.sum(grad_rows * by_rows, axis=1, keepdims=True))
    grad_scores = grad_scores + by_cols * (grad_cols - jnp.sum(grad_cols * by_cols, axis=0, keepdims=True))
    score_half = (score_scale * grad_scores).astype(jnp.bfloat16)
    return cols_half, grad_warp, score_half, residual


def reference(queries, keys):
    frames = queries.shape[0]
    score_scale = queries.shape[2] ** -0.5

    def add_pair(pair_index, totals):
        grad_q, grad_k = totals
        source_at = pair_index // frames
        target_at = pair_index % frames
        query_frame = lax.dynamic_index_in_dim(queries, source_at, 0, False)
        key_frame = lax.dynamic_index_in_dim(keys, target_at, 0, False)
        cols_half, grad_warp, score_half, residual = cycle_terms(query_frame, key_frame, score_scale, frames)
        q_term = jnp.dot(cols_half, grad_warp, preferred_element_type=jnp.float32)
        q_term = q_term + jnp.dot(score_half, key_frame, preferred_element_type=jnp.float32) - residual
        k_term = contract(score_half, query_frame, 0, 0)
        return grad_q.at[source_at].add(q_term), grad_k.at[target_at].add(k_term)

    empty_q = jnp.zeros(queries.shape, jnp.float32)
    empty_k = jnp.zeros(keys.shape, jnp.float32)
    grad_q, grad_k = lax.fori_loop(0, frames * frames, add_pair, (empty_q, empty_k))
    return grad_q, grad_k
```

```python
import jax
import jax.numpy as jnp
from jax import lax
from jax.experimental import pallas as pl
from jax.experimental.pallas import tpu as pltpu
from jax.sharding import PartitionSpec as P

MESH = pl.DeviceIdType.MESH
BF16 = jnp.bfloat16
F32 = jnp.float32


def contract(left_side, right_side, left_dim, right_dim):
    return lax.dot_general(
        left_side,
        right_side,
        (((left_dim,), (right_dim,)), ((), ())),
        preferred_element_type=jnp.float32,
    )


def cycle_terms(query_frame, key_frame, score_scale, frames):
    scores = score_scale * contract(query_frame, key_frame, 1, 1)
    by_rows = jax.nn.softmax(scores, axis=1)
    by_cols = jax.nn.softmax(scores, axis=0)
    rows_half = by_rows.astype(jnp.bfloat16)
    cols_half = by_cols.astype(jnp.bfloat16)
    warped = contract(cols_half, query_frame, 0, 0).astype(jnp.bfloat16)
    cycled = jnp.dot(rows_half, warped, preferred_element_type=jnp.float32)
    residual = (cycled - query_frame.astype(jnp.float32)) / frames
    resid_half = residual.astype(jnp.bfloat16)
    grad_rows = contract(resid_half, warped, 1, 1)
    grad_warp = contract(rows_half, resid_half, 0, 0).astype(jnp.bfloat16)
    grad_cols = contract(query_frame, grad_warp, 1, 1)
    grad_scores = by_rows * (grad_rows - jnp.sum(grad_rows * by_rows, axis=1, keepdims=True))
    grad_scores = grad_scores + by_cols * (
        grad_cols - jnp.sum(grad_cols * by_cols, axis=0, keepdims=True)
    )
    score_half = (score_scale * grad_scores).astype(jnp.bfloat16)
    return (cols_half, grad_warp, score_half, residual)


class Place:
    def __init__(self):
        row = lax.axis_index("row")
        col = lax.axis_index("col")
        self.zh, self.x = row // 4, row % 4
        self.y, self.zl, self.c = col // 4, (col // 2) % 2, col % 2
        self.row, self.col = row, col

    def at_x(self, step):
        return (self.zh * 4 + (self.x + step + 4) % 4, self.col)

    def at_zh(self, step):
        return (((self.zh + step + 4) % 4) * 4 + self.x, self.col)

    def at_y(self, step):
        return (self.row, ((self.y + step + 4) % 4) * 4 + self.zl * 2 + self.c)

    def at_zl(self):
        return (self.row, self.y * 4 + (1 - self.zl) * 2 + self.c)

    def at_core(self):
        return (self.row, self.y * 4 + self.zl * 2 + 1 - self.c)


def greet(at):
    barrier = pltpu.get_barrier_semaphore()
    for other in (
        at.at_core(),
        at.at_zl(),
        at.at_x(1),
        at.at_x(-1),
        at.at_y(1),
        at.at_y(-1),
        at.at_zh(1),
        at.at_zh(-1),
    ):
        pl.semaphore_signal(barrier, inc=1, device_id=other, device_id_type=MESH)
    pl.semaphore_wait(barrier, 8)


class Sends:
    def __init__(self, send_sem):
        self.send_sem = send_sem
        self.started = []

    def go(self, src, dst, recv, device):
        copy = pltpu.make_async_remote_copy(
            src_ref=src,
            dst_ref=dst,
            send_sem=self.send_sem.at[len(self.started)],
            recv_sem=recv,
            device_id=device,
            device_id_type=MESH,
        )
        copy.start()
        self.started.append(copy)

    def finish(self):
        for copy in self.started:
            copy.wait_send()


def kslot(dx, dz):
    return (dx % 4) * 4 + dz % 4


def qslot(dy, dzl, dc):
    return ((dy % 4) * 2 + dzl) * 2 + dc


def gather_kernel(q_ref, k_ref, qf, kf, send_sem, q_sem, k_sem):
    at = Place()
    s = 1 - 2 * at.c
    low = 3 - 2 * at.c
    high = 1 + 2 * at.c
    greet(at)
    out = Sends(send_sem)

    def got_k(dx, dz):
        slot = kslot(dx, dz)
        pltpu.make_async_remote_copy(
            src_ref=kf.at[slot], dst_ref=kf.at[slot], send_sem=send_sem.at[0],
            recv_sem=k_sem.at[slot], device_id=at.at_core(), device_id_type=MESH,
        ).wait_recv()

    def got_q(dy, dzl, dc):
        slot = qslot(dy, dzl, dc)
        pltpu.make_async_remote_copy(
            src_ref=qf.at[slot], dst_ref=qf.at[slot], send_sem=send_sem.at[0],
            recv_sem=q_sem.at[slot], device_id=at.at_core(), device_id_type=MESH,
        ).wait_recv()

    def send_k(src, slot, device):
        out.go(src, kf.at[slot], k_sem.at[slot], device)

    def send_q(src, slot, device):
        out.go(src, qf.at[slot], q_sem.at[slot], device)

    def k_along_x(src, dz):
        send_k(src, kslot(3, dz), at.at_x(1))
        send_k(src, kslot(1, dz), at.at_x(-1))

    def k_relay_x(dz):
        if dz % 2 == 0:
            send_k(kf.at[low * 4 + dz], kslot(2, dz), at.at_x(s))
        else:
            send_k(kf.at[high * 4 + dz], kslot(2, dz), at.at_x(-s))

    def q_along_y(src, dzl):
        send_q(src, qslot(3, dzl, 0), at.at_y(1))
        send_q(src, qslot(1, dzl, 0), at.at_y(-1))

    def q_relay_y(dzl):
        if dzl == 0:
            send_q(qf.at[low * 4 + dzl * 2], qslot(2, dzl, 0), at.at_y(s))
        else:
            send_q(qf.at[high * 4 + dzl * 2], qslot(2, dzl, 0), at.at_y(-s))

    def q_to_core(src, dy, dzl):
        send_q(src, qslot(dy, dzl, 1), at.at_core())

    send_q(q_ref, qslot(0, 1, 0), at.at_zl())
    send_k(k_ref, kslot(0, 3), at.at_zh(1))
    send_k(k_ref, kslot(0, 1), at.at_zh(-1))
    k_along_x(k_ref, 0)
    q_along_y(q_ref, 0)
    q_to_core(q_ref, 0, 0)
    kf[kslot(0, 0)] = k_ref[...]
    qf[qslot(0, 0, 0)] = q_ref[...]

    got_q(0, 1, 0)
    q_along_y(qf.at[qslot(0, 1, 0)], 1)
    q_to_core(qf.at[qslot(0, 1, 0)], 0, 1)

    got_k(3, 0)
    got_k(1, 0)
    k_relay_x(0)

    got_q(3, 0, 0)
    got_q(1, 0, 0)
    q_relay_y(0)
    q_to_core(qf.at[qslot(3, 0, 0)], 3, 0)
    q_to_core(qf.at[qslot(1, 0, 0)], 1, 0)

    got_k(0, 3)
    got_k(0, 1)
    send_k(kf.at[low], kslot(0, 2), at.at_zh(s))
    k_along_x(kf.at[kslot(0, 1)], 1)
    k_along_x(kf.at[kslot(0, 3)], 3)

    got_q(3, 1, 0)
    got_q(1, 1, 0)
    q_relay_y(1)
    q_to_core(qf.at[qslot(3, 1, 0)], 3, 1)
    q_to_core(qf.at[qslot(1, 1, 0)], 1, 1)

    got_q(2, 0, 0)
    q_to_core(qf.at[qslot(2, 0, 0)], 2, 0)

    got_k(0, 2)
    k_along_x(kf.at[kslot(0, 2)], 2)

    got_q(2, 1, 0)
    q_to_core(qf.at[qslot(2, 1, 0)], 2, 1)

    for dz in (1, 3):
        got_k(3, dz)
        got_k(1, dz)
        k_relay_x(dz)
    got_k(3, 2)
    got_k(1, 2)
    k_relay_x(2)

    for dz in (0, 1, 3, 2):
        got_k(2, dz)
    for dy in (0, 1, 3, 2):
        for dzl in (0, 1):
            got_q(dy, dzl, 1)
    out.finish()


def gather(queries, keys):
    rows, width = queries.shape
    full = jax.ShapeDtypeStruct((16, rows, width), BF16)
    vmem = pl.BlockSpec(memory_space=pltpu.VMEM)
    return pl.pallas_call(
        gather_kernel,
        out_shape=(full, full),
        in_specs=[vmem, vmem],
        out_specs=(vmem, vmem),
        scratch_shapes=[
            pltpu.SemaphoreType.DMA((32,)),
            pltpu.SemaphoreType.DMA((16,)),
            pltpu.SemaphoreType.DMA((16,)),
        ],
        compiler_params=pltpu.CompilerParams(
            collective_id=0, has_side_effects=True, vmem_limit_bytes=32 * 2**20
        ),
        name="gather_frames",
    )(queries, keys)


def reduce_kernel(
    qp, kp, q_out, k_out,
    kstage, kopp, kin, kzst, kzopp, kzin,
    qcst, qcin, qsum, qstage, qopp, qin, qzst, qzin,
    send_sem, kopp_sem, kin_sem, kz_sem, qc_sem, qopp_sem, qin_sem, qz_sem,
):
    at = Place()
    s = 1 - 2 * at.c
    low = 3 - 2 * at.c
    high = 1 + 2 * at.c
    greet(at)
    out = Sends(send_sem)

    def got(ref, sem):
        pltpu.make_async_remote_copy(
            src_ref=ref, dst_ref=ref, send_sem=send_sem.at[0],
            recv_sem=sem, device_id=at.at_core(), device_id_type=MESH,
        ).wait_recv()

    for dy in (2, 1, 3, 0):
        for dzl in (1, 0):
            slot = dy * 2 + dzl
            qcst[slot] = qp[qslot(dy, dzl, 1)].astype(BF16)
            out.go(qcst.at[slot], qcin.at[slot], qc_sem.at[slot], at.at_core())

    for dz in (2, 1, 3, 0):
        kstage[kslot(2, dz)] = kp[kslot(2, dz)].astype(BF16)
        out.go(kstage.at[kslot(2, dz)], kopp.at[dz], kopp_sem.at[dz], at.at_x(s if dz % 2 == 0 else -s))
    for dz in (2, 1, 3, 0):
        if dz % 2 == 0:
            slot = low * 4 + dz
            kstage[slot] = kp[slot].astype(BF16)
            out.go(kstage.at[slot], kin.at[4 + dz], kin_sem.at[4 + dz], at.at_x(-s))
        else:
            slot = high * 4 + dz
            kstage[slot] = kp[slot].astype(BF16)
            out.go(kstage.at[slot], kin.at[dz], kin_sem.at[dz], at.at_x(s))

    def core_sum(dy, dzl):
        slot = dy * 2 + dzl
        got(qcin.at[slot], qc_sem.at[slot])
        qsum[slot] = qp[qslot(dy, dzl, 0)] + qcin[slot].astype(F32)

    for dzl in (1, 0):
        core_sum(2, dzl)
        slot = 4 + dzl
        qstage[slot] = qsum[slot].astype(BF16)
        out.go(qstage.at[slot], qopp.at[dzl], qopp_sem.at[dzl], at.at_y(s if dzl == 0 else -s))
    for dy in (1, 3):
        for dzl in (1, 0):
            core_sum(dy, dzl)
    slot = high * 2 + 1
    qstage[slot] = qsum[slot].astype(BF16)
    out.go(qstage.at[slot], qin.at[1], qin_sem.at[1], at.at_y(s))
    slot = low * 2
    qstage[slot] = qsum[slot].astype(BF16)
    out.go(qstage.at[slot], qin.at[2], qin_sem.at[2], at.at_y(-s))

    for dz in (2, 1, 3, 0):
        got(kopp.at[dz], kopp_sem.at[dz])
        if dz % 2 == 0:
            slot = high * 4 + dz
            kstage[slot] = (kp[slot] + kopp[dz].astype(F32)).astype(BF16)
            out.go(kstage.at[slot], kin.at[dz], kin_sem.at[dz], at.at_x(s))
        else:
            slot = low * 4 + dz
            kstage[slot] = (kp[slot] + kopp[dz].astype(F32)).astype(BF16)
            out.go(kstage.at[slot], kin.at[4 + dz], kin_sem.at[4 + dz], at.at_x(-s))

    got(qopp.at[1], qopp_sem.at[1])
    slot = low * 2 + 1
    qstage[slot] = (qsum[slot] + qopp[1].astype(F32)).astype(BF16)
    out.go(qstage.at[slot], qin.at[3], qin_sem.at[3], at.at_y(-s))
    got(qopp.at[0], qopp_sem.at[0])
    slot = high * 2
    qstage[slot] = (qsum[slot] + qopp[0].astype(F32)).astype(BF16)
    out.go(qstage.at[slot], qin.at[0], qin_sem.at[0], at.at_y(s))

    core_sum(0, 1)
    core_sum(0, 0)
    got(qin.at[1], qin_sem.at[1])
    got(qin.at[3], qin_sem.at[3])
    qzst[...] = (qsum[1] + qin[1].astype(F32) + qin[3].astype(F32)).astype(BF16)
    out.go(qzst, qzin, qz_sem.at[0], at.at_zl())

    def k_sum(slot, dz):
        return kp[slot] + kin[dz].astype(F32) + kin[4 + dz].astype(F32)

    def k_ready(dz):
        got(kin.at[dz], kin_sem.at[dz])
        got(kin.at[4 + dz], kin_sem.at[4 + dz])

    k_ready(2)
    kzst[2] = k_sum(2, 2).astype(BF16)
    out.go(kzst.at[2], kzopp, kz_sem.at[2], at.at_zh(s))
    k_ready(1)
    k_ready(3)
    kzst[1] = k_sum(low, low).astype(BF16)
    out.go(kzst.at[1], kzin.at[1], kz_sem.at[1], at.at_zh(-s))
    ahead = k_sum(high, high)
    got(kzopp, kz_sem.at[2])
    kzst[0] = (ahead + kzopp[...].astype(F32)).astype(BF16)
    out.go(kzst.at[0], kzin.at[0], kz_sem.at[0], at.at_zh(s))

    got(qin.at[0], qin_sem.at[0])
    got(qin.at[2], qin_sem.at[2])
    got(qzin, qz_sem.at[0])
    q_out[...] = (qsum[0] + qin[0].astype(F32) + qin[2].astype(F32)) + qzin[...].astype(F32)

    k_ready(0)
    total = k_sum(0, 0)
    got(kzin.at[0], kz_sem.at[0])
    got(kzin.at[1], kz_sem.at[1])
    k_out[...] = total + kzin[0].astype(F32) + kzin[1].astype(F32)
    out.finish()


def reduce_scatter(q_terms, k_terms):
    _, rows, width = q_terms.shape
    vmem = pl.BlockSpec(memory_space=pltpu.VMEM)
    own = jax.ShapeDtypeStruct((rows, width), F32)

    def buf(*lead, dtype=BF16):
        return pltpu.VMEM((*lead, rows, width), dtype)

    def sems(count):
        return pltpu.SemaphoreType.DMA((count,))

    return pl.pallas_call(
        reduce_kernel,
        out_shape=(own, own),
        in_specs=[vmem, vmem],
        out_specs=(vmem, vmem),
        scratch_shapes=[
            buf(16), buf(4), buf(8), buf(3), buf(), buf(2),
            buf(8), buf(8), buf(8, dtype=F32), buf(8), buf(2), buf(4), buf(), buf(),
            sems(32), sems(4), sems(8), sems(3), sems(8), sems(2), sems(4), sems(1),
        ],
        compiler_params=pltpu.CompilerParams(
            collective_id=1, has_side_effects=True, vmem_limit_bytes=48 * 2**20
        ),
        name="reduce_terms",
    )(q_terms, k_terms)


def local(queries, keys):
    frames = queries.shape[0] * lax.axis_size("row")
    _, rows, width = queries.shape
    whole_q, whole_k = gather(queries[0], keys[0])
    query_frame = whole_q.reshape(16 * rows, width)
    key_frame = whole_k.reshape(16 * rows, width)
    cols_half, grad_warp, score_half, residual = cycle_terms(
        query_frame, key_frame, width**-0.5, frames
    )
    q_term = jnp.dot(cols_half, grad_warp, preferred_element_type=jnp.float32)
    q_term = q_term + jnp.dot(score_half, key_frame, preferred_element_type=jnp.float32) - residual
    k_term = contract(score_half, query_frame, 0, 0)
    out_q, out_k = reduce_scatter(q_term.reshape(16, rows, width), k_term.reshape(16, rows, width))
    return (out_q[None], out_k[None])


def solution(mesh):
    placed = (P("row", "col", None), P("col", "row", None))
    return jax.shard_map(
        local,
        mesh=mesh,
        in_specs=placed,
        out_specs=(P("row", "col", None), P("col", "row", None)),
        check_vma=False,
    )
```

```python
import jax
import jax.numpy as jnp
from jax import lax
from jax.experimental import pallas as pl
from jax.experimental.pallas import tpu as pltpu
from jax.sharding import PartitionSpec as P

MESH = pl.DeviceIdType.MESH
BF16 = jnp.bfloat16
F32 = jnp.float32


def contract(left_side, right_side, left_dim, right_dim):
    return lax.dot_general(
        left_side,
        right_side,
        (((left_dim,), (right_dim,)), ((), ())),
        preferred_element_type=jnp.float32,
    )


def cycle_terms(query_frame, key_frame, score_scale, frames):
    scores = score_scale * contract(query_frame, key_frame, 1, 1)
    by_rows = jax.nn.softmax(scores, axis=1)
    by_cols = jax.nn.softmax(scores, axis=0)
    rows_half = by_rows.astype(jnp.bfloat16)
    cols_half = by_cols.astype(jnp.bfloat16)
    warped = contract(cols_half, query_frame, 0, 0).astype(jnp.bfloat16)
    cycled = jnp.dot(rows_half, warped, preferred_element_type=jnp.float32)
    residual = (cycled - query_frame.astype(jnp.float32)) / frames
    resid_half = residual.astype(jnp.bfloat16)
    grad_rows = contract(resid_half, warped, 1, 1)
    grad_warp = contract(rows_half, resid_half, 0, 0).astype(jnp.bfloat16)
    grad_cols = contract(query_frame, grad_warp, 1, 1)
    grad_scores = by_rows * (grad_rows - jnp.sum(grad_rows * by_rows, axis=1, keepdims=True))
    grad_scores = grad_scores + by_cols * (
        grad_cols - jnp.sum(grad_cols * by_cols, axis=0, keepdims=True)
    )
    score_half = (score_scale * grad_scores).astype(jnp.bfloat16)
    return (cols_half, grad_warp, score_half, residual)


class Place:
    def __init__(self):
        row = lax.axis_index("row")
        col = lax.axis_index("col")
        self.zh, self.x = row // 4, row % 4
        self.y, self.zl, self.c = col // 4, (col // 2) % 2, col % 2
        self.row, self.col = row, col

    def at_x(self, step):
        return (self.zh * 4 + (self.x + step + 4) % 4, self.col)

    def at_zh(self, step):
        return (((self.zh + step + 4) % 4) * 4 + self.x, self.col)

    def at_y(self, step):
        return (self.row, ((self.y + step + 4) % 4) * 4 + self.zl * 2 + self.c)

    def at_zl(self):
        return (self.row, self.y * 4 + (1 - self.zl) * 2 + self.c)

    def at_core(self):
        return (self.row, self.y * 4 + self.zl * 2 + 1 - self.c)


def greet(at):
    barrier = pltpu.get_barrier_semaphore()
    others = [at.at_core(), at.at_zl()]
    for step in (1, -1, 2):
        others += [at.at_x(step), at.at_y(step), at.at_zh(step)]
    for other in others:
        pl.semaphore_signal(barrier, inc=1, device_id=other, device_id_type=MESH)
    pl.semaphore_wait(barrier, len(others))


class Sends:
    def __init__(self, send_sem):
        self.send_sem = send_sem
        self.started = []

    def go(self, src, dst, recv, device):
        copy = pltpu.make_async_remote_copy(
            src_ref=src,
            dst_ref=dst,
            send_sem=self.send_sem.at[len(self.started)],
            recv_sem=recv,
            device_id=device,
            device_id_type=MESH,
        )
        copy.start()
        self.started.append(copy)

    def finish(self):
        for copy in self.started:
            copy.wait_send()


def kslot(dx, dz):
    return (dx % 4) * 4 + dz % 4


def qslot(dy, dzl, dc):
    return ((dy % 4) * 2 + dzl) * 2 + dc


def gather_kernel(q_ref, k_ref, qf, kf, send_sem, q_sem, k_sem):
    at = Place()
    greet(at)
    out = Sends(send_sem)

    def got(ref, sem):
        pltpu.make_async_remote_copy(
            src_ref=ref, dst_ref=ref, send_sem=send_sem.at[0],
            recv_sem=sem, device_id=at.at_core(), device_id_type=MESH,
        ).wait_recv()

    def got_k(dx, dz):
        slot = kslot(dx, dz)
        got(kf.at[slot], k_sem.at[slot])
        return kf.at[slot]

    def got_q(dy, dzl, dc):
        slot = qslot(dy, dzl, dc)
        got(qf.at[slot], q_sem.at[slot])
        return qf.at[slot]

    def k_along_x(src, dz, steps=(1, -1)):
        for step in steps:
            slot = kslot(-step, dz)
            out.go(src, kf.at[slot], k_sem.at[slot], at.at_x(step))

    def k_along_z(src, dx, steps=(1, -1)):
        for step in steps:
            slot = kslot(dx, -step)
            out.go(src, kf.at[slot], k_sem.at[slot], at.at_zh(step))

    def q_along_y(src, dzl):
        for step in (1, -1, 2):
            slot = qslot(-step, dzl, 0)
            out.go(src, qf.at[slot], q_sem.at[slot], at.at_y(step))

    def q_to_core(src, dy, dzl):
        slot = qslot(dy, dzl, 1)
        out.go(src, qf.at[slot], q_sem.at[slot], at.at_core())

    slot = qslot(0, 1, 0)
    out.go(q_ref, qf.at[slot], q_sem.at[slot], at.at_zl())
    k_along_z(k_ref, 0)
    k_along_x(k_ref, 0)
    q_along_y(q_ref, 0)
    k_along_z(k_ref, 0, (2,))
    k_along_x(k_ref, 0, (2,))
    q_to_core(q_ref, 0, 0)
    kf[kslot(0, 0)] = k_ref[...]
    qf[qslot(0, 0, 0)] = q_ref[...]

    block = got_q(0, 1, 0)
    q_along_y(block, 1)
    q_to_core(block, 0, 1)

    k_along_x(got_k(0, 1), 1)
    k_along_x(got_k(0, 3), 3)
    for dy in (1, 3, 2):
        q_to_core(got_q(dy, 0, 0), dy, 0)
    k_along_z(got_k(2, 0), 2)
    block = got_k(0, 2)
    k_along_x(block, 2)
    k_along_x(block, 2, (2,))
    for dy in (1, 3, 2):
        q_to_core(got_q(dy, 1, 0), dy, 1)

    for dx, dz in ((1, 0), (3, 0), (1, 1), (3, 1), (1, 3), (3, 3), (2, 1), (2, 3), (1, 2), (3, 2), (2, 2)):
        got_k(dx, dz)
    for dy in (0, 1, 3, 2):
        for dzl in (0, 1):
            got_q(dy, dzl, 1)
    out.finish()


def gather(queries, keys):
    rows, width = queries.shape
    full = jax.ShapeDtypeStruct((16, rows, width), BF16)
    vmem = pl.BlockSpec(memory_space=pltpu.VMEM)
    return pl.pallas_call(
        gather_kernel,
        out_shape=(full, full),
        in_specs=[vmem, vmem],
        out_specs=(vmem, vmem),
        scratch_shapes=[
            pltpu.SemaphoreType.DMA((32,)),
            pltpu.SemaphoreType.DMA((16,)),
            pltpu.SemaphoreType.DMA((16,)),
        ],
        compiler_params=pltpu.CompilerParams(
            collective_id=0, has_side_effects=True, vmem_limit_bytes=32 * 2**20
        ),
        name="gather_frames",
    )(queries, keys)


def reduce_kernel(
    qp, kp, q_out, k_out,
    kst, kx1, kx2, kzt, kzin, qcst, qcin, qsum, qst, qyin, qzst, qzin,
    send_sem, kx1_sem, kx2_sem, kzt_sem, kzin_sem, qc_sem, qy_sem, qz_sem,
):
    at = Place()
    greet(at)
    out = Sends(send_sem)

    def got(ref, sem):
        pltpu.make_async_remote_copy(
            src_ref=ref, dst_ref=ref, send_sem=send_sem.at[0],
            recv_sem=sem, device_id=at.at_core(), device_id_type=MESH,
        ).wait_recv()

    def send_k(dx, dz, dst, sem, device):
        slot = kslot(dx, dz)
        kst[slot] = kp[slot].astype(BF16)
        out.go(kst.at[slot], dst, sem, device)

    send_k(2, 1, kzt.at[0], kzt_sem.at[0], at.at_zh(1))
    send_k(2, 3, kzt.at[1], kzt_sem.at[1], at.at_zh(-1))
    send_k(2, 2, kx2.at[1], kx2_sem.at[1], at.at_x(2))
    for dz in (2, 1, 3, 0):
        send_k(1, dz, kx1.at[dz], kx1_sem.at[dz], at.at_x(1))
        send_k(3, dz, kx1.at[4 + dz], kx1_sem.at[4 + dz], at.at_x(-1))
    for dzl in (1, 0):
        for dy in (2, 1, 3, 0):
            slot = dy * 2 + dzl
            qcst[slot] = qp[qslot(dy, dzl, 1)].astype(BF16)
            out.go(qcst.at[slot], qcin.at[slot], qc_sem.at[slot], at.at_core())

    def core_sum(dy, dzl):
        slot = dy * 2 + dzl
        got(qcin.at[slot], qc_sem.at[slot])
        return qp[qslot(dy, dzl, 0)] + qcin[slot].astype(F32)

    for dzl in (1, 0):
        for dy in (2, 1, 3):
            slot = dy * 2 + dzl
            qst[slot] = core_sum(dy, dzl).astype(BF16)
            out.go(qst.at[slot], qyin.at[slot], qy_sem.at[slot], at.at_y(dy if dy < 3 else -1))
        qsum[dzl] = core_sum(0, dzl)

    for side in (0, 1):
        got(kzt.at[side], kzt_sem.at[side])
    kst[kslot(2, 0)] = (kp[kslot(2, 0)] + kzt[0].astype(F32) + kzt[1].astype(F32)).astype(BF16)
    out.go(kst.at[kslot(2, 0)], kx2.at[0], kx2_sem.at[0], at.at_x(2))

    def k_sum(dz):
        got(kx1.at[dz], kx1_sem.at[dz])
        got(kx1.at[4 + dz], kx1_sem.at[4 + dz])
        return kp[kslot(0, dz)] + kx1[dz].astype(F32) + kx1[4 + dz].astype(F32)

    total = k_sum(2)
    got(kx2.at[1], kx2_sem.at[1])
    kst[2] = (total + kx2[1].astype(F32)).astype(BF16)
    out.go(kst.at[2], kzin.at[2], kzin_sem.at[2], at.at_zh(2))
    for dz in (1, 3):
        kst[dz] = k_sum(dz).astype(BF16)
        out.go(kst.at[dz], kzin.at[dz], kzin_sem.at[dz], at.at_zh(dz if dz < 3 else -1))

    def y_sum(dzl):
        total = qsum[dzl]
        for dy in (1, 3, 2):
            slot = dy * 2 + dzl
            got(qyin.at[slot], qy_sem.at[slot])
            total = total + qyin[slot].astype(F32)
        return total

    qzst[...] = y_sum(1).astype(BF16)
    out.go(qzst, qzin, qz_sem.at[0], at.at_zl())
    qsum[0] = y_sum(0)

    total = k_sum(0)
    got(kx2.at[0], kx2_sem.at[0])
    total = total + kx2[0].astype(F32)
    got(qzin, qz_sem.at[0])
    q_out[...] = qsum[0] + qzin[...].astype(F32)
    for dz in (1, 3, 2):
        got(kzin.at[dz], kzin_sem.at[dz])
        total = total + kzin[dz].astype(F32)
    k_out[...] = total
    out.finish()


def reduce_scatter(q_terms, k_terms):
    _, rows, width = q_terms.shape
    vmem = pl.BlockSpec(memory_space=pltpu.VMEM)
    own = jax.ShapeDtypeStruct((rows, width), F32)

    def buf(*lead, dtype=BF16):
        return pltpu.VMEM((*lead, rows, width), dtype)

    def sems(count):
        return pltpu.SemaphoreType.DMA((count,))

    return pl.pallas_call(
        reduce_kernel,
        out_shape=(own, own),
        in_specs=[vmem, vmem],
        out_specs=(vmem, vmem),
        scratch_shapes=[
            buf(16), buf(8), buf(2), buf(2), buf(4),
            buf(8), buf(8), buf(2, dtype=F32), buf(8), buf(8), buf(), buf(),
            sems(32), sems(8), sems(2), sems(2), sems(4), sems(8), sems(8), sems(1),
        ],
        compiler_params=pltpu.CompilerParams(
            collective_id=1, has_side_effects=True, vmem_limit_bytes=48 * 2**20
        ),
        name="reduce_terms",
    )(q_terms, k_terms)


def local(queries, keys):
    frames = queries.shape[0] * lax.axis_size("row")
    _, rows, width = queries.shape
    whole_q, whole_k = gather(queries[0], keys[0])
    query_frame = whole_q.reshape(16 * rows, width)
    key_frame = whole_k.reshape(16 * rows, width)
    cols_half, grad_warp, score_half, residual = cycle_terms(
        query_frame, key_frame, width**-0.5, frames
    )
    q_term = jnp.dot(cols_half, grad_warp, preferred_element_type=jnp.float32)
    q_term = q_term + jnp.dot(score_half, key_frame, preferred_element_type=jnp.float32) - residual
    k_term = contract(score_half, query_frame, 0, 0)
    out_q, out_k = reduce_scatter(q_term.reshape(16, rows, width), k_term.reshape(16, rows, width))
    return (out_q[None], out_k[None])


def solution(mesh):
    placed = (P("row", "col", None), P("col", "row", None))
    return jax.shard_map(
        local,
        mesh=mesh,
        in_specs=placed,
        out_specs=(P("row", "col", None), P("col", "row", None)),
        check_vma=False,
    )
```

```python
import functools
import math

import jax
import jax.numpy as jnp
from jax import lax
from jax.experimental import pallas as pl
from jax.experimental.pallas import tpu as pltpu
from jax.sharding import PartitionSpec as P

MESH = pl.DeviceIdType.MESH
BF16 = jnp.bfloat16
F32 = jnp.float32


class Place:
    def __init__(self):
        row = lax.axis_index("row")
        col = lax.axis_index("col")
        self.zh, self.x = row // 4, row % 4
        self.y, self.zl, self.c = col // 4, (col // 2) % 2, col % 2
        self.row, self.col = row, col

    def at_x(self, step):
        return (self.zh * 4 + (self.x + step + 4) % 4, self.col)

    def at_zh(self, step):
        return (((self.zh + step + 4) % 4) * 4 + self.x, self.col)

    def at_y(self, step):
        return (self.row, ((self.y + step + 4) % 4) * 4 + self.zl * 2 + self.c)

    def at_zl(self):
        return (self.row, self.y * 4 + (1 - self.zl) * 2 + self.c)

    def at_core(self):
        return (self.row, self.y * 4 + self.zl * 2 + 1 - self.c)


def greet(at):
    barrier = pltpu.get_barrier_semaphore()
    others = [at.at_core(), at.at_zl()]
    for step in (1, -1, 2):
        others += [at.at_x(step), at.at_y(step), at.at_zh(step)]
    for other in others:
        pl.semaphore_signal(barrier, inc=1, device_id=other, device_id_type=MESH)
    pl.semaphore_wait(barrier, len(others))


class Sends:
    def __init__(self, send_sem):
        self.send_sem = send_sem
        self.started = []

    def go(self, src, dst, recv, device):
        copy = pltpu.make_async_remote_copy(
            src_ref=src,
            dst_ref=dst,
            send_sem=self.send_sem.at[len(self.started)],
            recv_sem=recv,
            device_id=device,
            device_id_type=MESH,
        )
        copy.start()
        self.started.append(copy)

    def finish(self):
        for copy in self.started:
            copy.wait_send()


def kslot(dx, dz):
    return (dx % 4) * 4 + dz % 4


def qslot(dy, dzl, dc):
    return ((dy % 4) * 2 + dzl) * 2 + dc


def gather_kernel(q_ref, k_ref, qf, kf, send_sem, q_sem, k_sem):
    at = Place()
    greet(at)
    out = Sends(send_sem)

    def got(ref, sem):
        pltpu.make_async_remote_copy(
            src_ref=ref, dst_ref=ref, send_sem=send_sem.at[0],
            recv_sem=sem, device_id=at.at_core(), device_id_type=MESH,
        ).wait_recv()

    def got_k(dx, dz):
        slot = kslot(dx, dz)
        got(kf.at[slot], k_sem.at[slot])
        return kf.at[slot]

    def got_q(dy, dzl, dc):
        slot = qslot(dy, dzl, dc)
        got(qf.at[slot], q_sem.at[slot])
        return qf.at[slot]

    def k_along_x(src, dz, steps=(1, -1)):
        for step in steps:
            slot = kslot(-step, dz)
            out.go(src, kf.at[slot], k_sem.at[slot], at.at_x(step))

    def k_along_z(src, dx, steps=(1, -1)):
        for step in steps:
            slot = kslot(dx, -step)
            out.go(src, kf.at[slot], k_sem.at[slot], at.at_zh(step))

    def q_along_y(src, dzl):
        for step in (1, -1, 2):
            slot = qslot(-step, dzl, 0)
            out.go(src, qf.at[slot], q_sem.at[slot], at.at_y(step))

    def q_to_core(src, dy, dzl):
        slot = qslot(dy, dzl, 1)
        out.go(src, qf.at[slot], q_sem.at[slot], at.at_core())

    slot = qslot(0, 1, 0)
    out.go(q_ref, qf.at[slot], q_sem.at[slot], at.at_zl())
    k_along_z(k_ref, 0)
    k_along_x(k_ref, 0)
    q_along_y(q_ref, 0)
    k_along_z(k_ref, 0, (2,))
    k_along_x(k_ref, 0, (2,))
    q_to_core(q_ref, 0, 0)
    kf[kslot(0, 0)] = k_ref[...]
    qf[qslot(0, 0, 0)] = q_ref[...]

    block = got_q(0, 1, 0)
    q_along_y(block, 1)
    q_to_core(block, 0, 1)

    k_along_x(got_k(0, 1), 1)
    k_along_x(got_k(0, 3), 3)
    for dy in (1, 3, 2):
        q_to_core(got_q(dy, 0, 0), dy, 0)
    k_along_z(got_k(2, 0), 2)
    block = got_k(0, 2)
    k_along_x(block, 2)
    k_along_x(block, 2, (2,))
    for dy in (1, 3, 2):
        q_to_core(got_q(dy, 1, 0), dy, 1)

    for dx, dz in ((1, 0), (3, 0), (1, 1), (3, 1), (1, 3), (3, 3), (2, 1), (2, 3), (1, 2), (3, 2), (2, 2)):
        got_k(dx, dz)
    for dy in (0, 1, 3, 2):
        for dzl in (0, 1):
            got_q(dy, dzl, 1)
    out.finish()


def gather(queries, keys):
    rows, width = queries.shape
    full = jax.ShapeDtypeStruct((16, rows, width), BF16)
    vmem = pl.BlockSpec(memory_space=pltpu.VMEM)
    return pl.pallas_call(
        gather_kernel,
        out_shape=(full, full),
        in_specs=[vmem, vmem],
        out_specs=(vmem, vmem),
        scratch_shapes=[
            pltpu.SemaphoreType.DMA((32,)),
            pltpu.SemaphoreType.DMA((16,)),
            pltpu.SemaphoreType.DMA((16,)),
        ],
        compiler_params=pltpu.CompilerParams(
            collective_id=0, has_side_effects=True, vmem_limit_bytes=32 * 2**20
        ),
        name="gather_frames",
    )(queries, keys)


def reduce_kernel(
    qp, kp, q_out, k_out,
    kst, kx1, kx2, kzt, kzin, qcst, qcin, qsum, qst, qyin, qzst, qzin,
    send_sem, kx1_sem, kx2_sem, kzt_sem, kzin_sem, qc_sem, qy_sem, qz_sem,
):
    at = Place()
    greet(at)
    out = Sends(send_sem)

    def got(ref, sem):
        pltpu.make_async_remote_copy(
            src_ref=ref, dst_ref=ref, send_sem=send_sem.at[0],
            recv_sem=sem, device_id=at.at_core(), device_id_type=MESH,
        ).wait_recv()

    def send_k(dx, dz, dst, sem, device):
        slot = kslot(dx, dz)
        kst[slot] = kp[slot].astype(BF16)
        out.go(kst.at[slot], dst, sem, device)

    send_k(2, 1, kzt.at[0], kzt_sem.at[0], at.at_zh(1))
    send_k(2, 3, kzt.at[1], kzt_sem.at[1], at.at_zh(-1))
    send_k(2, 2, kx2.at[1], kx2_sem.at[1], at.at_x(2))
    for dz in (2, 1, 3, 0):
        send_k(1, dz, kx1.at[dz], kx1_sem.at[dz], at.at_x(1))
        send_k(3, dz, kx1.at[4 + dz], kx1_sem.at[4 + dz], at.at_x(-1))
    for dzl in (1, 0):
        for dy in (2, 1, 3, 0):
            slot = dy * 2 + dzl
            qcst[slot] = qp[qslot(dy, dzl, 1)].astype(BF16)
            out.go(qcst.at[slot], qcin.at[slot], qc_sem.at[slot], at.at_core())

    def core_sum(dy, dzl):
        slot = dy * 2 + dzl
        got(qcin.at[slot], qc_sem.at[slot])
        return qp[qslot(dy, dzl, 0)] + qcin[slot].astype(F32)

    for dzl in (1, 0):
        for dy in (2, 1, 3):
            slot = dy * 2 + dzl
            qst[slot] = core_sum(dy, dzl).astype(BF16)
            out.go(qst.at[slot], qyin.at[slot], qy_sem.at[slot], at.at_y(dy if dy < 3 else -1))
        qsum[dzl] = core_sum(0, dzl)

    for side in (0, 1):
        got(kzt.at[side], kzt_sem.at[side])
    kst[kslot(2, 0)] = (kp[kslot(2, 0)] + kzt[0].astype(F32) + kzt[1].astype(F32)).astype(BF16)
    out.go(kst.at[kslot(2, 0)], kx2.at[0], kx2_sem.at[0], at.at_x(2))

    def k_sum(dz):
        got(kx1.at[dz], kx1_sem.at[dz])
        got(kx1.at[4 + dz], kx1_sem.at[4 + dz])
        return kp[kslot(0, dz)] + kx1[dz].astype(F32) + kx1[4 + dz].astype(F32)

    total = k_sum(2)
    got(kx2.at[1], kx2_sem.at[1])
    kst[2] = (total + kx2[1].astype(F32)).astype(BF16)
    out.go(kst.at[2], kzin.at[2], kzin_sem.at[2], at.at_zh(2))
    for dz in (1, 3):
        kst[dz] = k_sum(dz).astype(BF16)
        out.go(kst.at[dz], kzin.at[dz], kzin_sem.at[dz], at.at_zh(dz if dz < 3 else -1))

    def y_sum(dzl):
        total = qsum[dzl]
        for dy in (1, 3, 2):
            slot = dy * 2 + dzl
            got(qyin.at[slot], qy_sem.at[slot])
            total = total + qyin[slot].astype(F32)
        return total

    qzst[...] = y_sum(1).astype(BF16)
    out.go(qzst, qzin, qz_sem.at[0], at.at_zl())
    qsum[0] = y_sum(0)

    total = k_sum(0)
    got(kx2.at[0], kx2_sem.at[0])
    total = total + kx2[0].astype(F32)
    got(qzin, qz_sem.at[0])
    q_out[...] = qsum[0] + qzin[...].astype(F32)
    for dz in (1, 3, 2):
        got(kzin.at[dz], kzin_sem.at[dz])
        total = total + kzin[dz].astype(F32)
    k_out[...] = total
    out.finish()


def reduce_scatter(q_terms, k_terms):
    _, rows, width = q_terms.shape
    vmem = pl.BlockSpec(memory_space=pltpu.VMEM)
    own = jax.ShapeDtypeStruct((rows, width), F32)

    def buf(*lead, dtype=BF16):
        return pltpu.VMEM((*lead, rows, width), dtype)

    def sems(count):
        return pltpu.SemaphoreType.DMA((count,))

    return pl.pallas_call(
        reduce_kernel,
        out_shape=(own, own),
        in_specs=[vmem, vmem],
        out_specs=(vmem, vmem),
        scratch_shapes=[
            buf(16), buf(8), buf(2), buf(2), buf(4),
            buf(8), buf(8), buf(2, dtype=F32), buf(8), buf(8), buf(), buf(),
            sems(32), sems(8), sems(2), sems(2), sems(4), sems(8), sems(8), sems(1),
        ],
        compiler_params=pltpu.CompilerParams(
            collective_id=1, has_side_effects=True, vmem_limit_bytes=48 * 2**20
        ),
        name="reduce_terms",
    )(q_terms, k_terms)


TOK = 768
KC = 192


def nt(a, b):
    return lax.dot_general(a, b, (((1,), (1,)), ((), ())), preferred_element_type=F32)


def nn(a, b):
    return lax.dot_general(a, b, (((1,), (0,)), ((), ())), preferred_element_type=F32)


def tn(a, b):
    return lax.dot_general(a, b, (((0,), (0,)), ((), ())), preferred_element_type=F32)


def fold(x, op):
    return op(x.reshape(x.shape[0] // 8, 8, x.shape[1]), axis=0)


class Pair:
    def __init__(self, scale, frames, qf, kf, st, bt, at, bh, ah, v, gr, gh, da, dv, ds, cmax, csum, cdel):
        self.__dict__.update(locals())

    def scores(self, c):
        rows = pl.ds(c * KC, KC)
        st = nt(self.kf[rows], self.qf[...]) * (self.scale * math.log2(math.e))
        self.st[rows] = st
        top = fold(st, jnp.max)
        self.cmax[...] = top if c == 0 else jnp.maximum(self.cmax[...], top)
        e = jnp.exp2(st - jnp.max(st, axis=1, keepdims=True))
        b = e * (1.0 / jnp.sum(e, axis=1, keepdims=True))
        self.bt[rows] = b
        bh = b.astype(BF16)
        self.bh[rows] = bh
        self.v[rows] = nn(bh, self.qf[...]).astype(BF16)

    def attend(self):
        top = jnp.max(self.cmax[...], axis=0, keepdims=True)
        total = jnp.zeros((8, TOK), F32)
        for c in range(TOK // KC):
            rows = pl.ds(c * KC, KC)
            e = jnp.exp2(self.st[rows] - top)
            self.at[rows] = e
            total = total + fold(e, jnp.sum)
        inv = 1.0 / jnp.sum(total, axis=0, keepdims=True)
        for c in range(TOK // KC):
            rows = pl.ds(c * KC, KC)
            a = self.at[rows] * inv
            self.at[rows] = a
            self.ah[rows] = a.astype(BF16)

    def residual(self, size=384):
        for c in range(TOK // size):
            rows = pl.ds(c * size, size)
            cycled = tn(self.ah[:, rows], self.v[...])
            g = (cycled - self.qf[rows].astype(F32)) * (1.0 / self.frames)
            self.gr[rows] = g
            self.gh[rows] = g.astype(BF16)

    def grad_rows(self, size=384):
        total = jnp.zeros((8, TOK), F32)
        for c in range(TOK // size):
            rows = pl.ds(c * size, size)
            da = nt(self.v[rows], self.gh[...])
            self.da[rows] = da
            total = total + fold(da * self.at[rows], jnp.sum)
        self.cdel[...] = jnp.broadcast_to(jnp.sum(total, axis=0, keepdims=True), (8, TOK))

    def grad_warp(self, size=384):
        for c in range(TOK // size):
            rows = pl.ds(c * size, size)
            self.dv[rows] = nn(self.ah[rows], self.gh[...]).astype(BF16)

    def grad_scores(self, c, size=KC):
        rows = pl.ds(c * size, size)
        db = nt(self.dv[rows], self.qf[...])
        b = self.bt[rows]
        delta = jnp.sum(db * b, axis=1, keepdims=True)
        ds = self.at[rows] * (self.da[rows] - self.cdel[0:1]) + b * (db - delta)
        dsh = (ds * self.scale).astype(BF16)
        self.ds[rows] = dsh
        return nn(dsh, self.qf[...])

    def query_terms(self, c, size=384):
        rows = pl.ds(c * size, size)
        return tn(self.bh[:, rows], self.dv[...]) + tn(self.ds[:, rows], self.kf[...]) - self.gr[rows]


def pair_scratch():
    def whole(dtype):
        return pltpu.VMEM((TOK, TOK), dtype)

    return [
        whole(F32), whole(F32), whole(F32), whole(BF16), whole(BF16), whole(BF16),
        whole(F32), whole(BF16), whole(F32), whole(BF16), whole(BF16),
        pltpu.VMEM((8, TOK), F32), pltpu.VMEM((8, TOK), F32), pltpu.VMEM((8, TOK), F32),
    ]


def pair_kernel(scale, frames, qf, kf, q_out, k_out, *scratch):
    pair = Pair(scale, frames, qf, kf, *scratch)
    for c in range(TOK // KC):
        pair.scores(c)
    pair.attend()
    pair.residual()
    pair.grad_rows()
    pair.grad_warp()
    for c in range(TOK // KC):
        k_out[pl.ds(c * KC, KC)] = pair.grad_scores(c)
    for c in range(2):
        q_out[pl.ds(c * 384, 384)] = pair.query_terms(c)


def pair_terms(whole_q, whole_k, scale, frames):
    vmem = pl.BlockSpec(memory_space=pltpu.VMEM)
    full = jax.ShapeDtypeStruct((TOK, TOK), F32)
    return pl.pallas_call(
        functools.partial(pair_kernel, scale, frames),
        out_shape=(full, full),
        in_specs=[vmem, vmem],
        out_specs=(vmem, vmem),
        scratch_shapes=pair_scratch(),
        compiler_params=pltpu.CompilerParams(vmem_limit_bytes=48 * 2**20),
        name="pair_terms",
    )(whole_q, whole_k)


def local(queries, keys):
    frames = queries.shape[0] * lax.axis_size("row")
    _, rows, width = queries.shape
    whole_q, whole_k = gather(queries[0], keys[0])
    q_term, k_term = pair_terms(
        whole_q.reshape(16 * rows, width), whole_k.reshape(16 * rows, width), width**-0.5, frames
    )
    out_q, out_k = reduce_scatter(q_term.reshape(16, rows, width), k_term.reshape(16, rows, width))
    return (out_q[None], out_k[None])


def solution(mesh):
    placed = (P("row", "col", None), P("col", "row", None))
    return jax.shard_map(
        local,
        mesh=mesh,
        in_specs=placed,
        out_specs=(P("row", "col", None), P("col", "row", None)),
        check_vma=False,
    )
```

```python
import functools
import math

import jax
import jax.numpy as jnp
from jax import lax
from jax.experimental import pallas as pl
from jax.experimental.pallas import tpu as pltpu
from jax.sharding import PartitionSpec as P

MESH = pl.DeviceIdType.MESH
BF16 = jnp.bfloat16
F32 = jnp.float32


class Place:
    def __init__(self):
        row = lax.axis_index("row")
        col = lax.axis_index("col")
        self.zh, self.x = row // 4, row % 4
        self.y, self.zl, self.c = col // 4, (col // 2) % 2, col % 2
        self.row, self.col = row, col

    def at_x(self, step):
        return (self.zh * 4 + (self.x + step + 4) % 4, self.col)

    def at_zh(self, step):
        return (((self.zh + step + 4) % 4) * 4 + self.x, self.col)

    def at_y(self, step):
        return (self.row, ((self.y + step + 4) % 4) * 4 + self.zl * 2 + self.c)

    def at_zl(self):
        return (self.row, self.y * 4 + (1 - self.zl) * 2 + self.c)

    def at_core(self):
        return (self.row, self.y * 4 + self.zl * 2 + 1 - self.c)


def greet(at):
    barrier = pltpu.get_barrier_semaphore()
    others = [at.at_core(), at.at_zl()]
    for step in (1, -1, 2):
        others += [at.at_x(step), at.at_y(step), at.at_zh(step)]
    for other in others:
        pl.semaphore_signal(barrier, inc=1, device_id=other, device_id_type=MESH)
    pl.semaphore_wait(barrier, len(others))


class Sends:
    def __init__(self, send_sem):
        self.send_sem = send_sem
        self.started = []

    def go(self, src, dst, recv, device):
        copy = pltpu.make_async_remote_copy(
            src_ref=src,
            dst_ref=dst,
            send_sem=self.send_sem.at[len(self.started)],
            recv_sem=recv,
            device_id=device,
            device_id_type=MESH,
        )
        copy.start()
        self.started.append(copy)

    def finish(self):
        for copy in self.started:
            copy.wait_send()


TOK = 768
ROWS = 48
KC = 192


def nt(a, b):
    return lax.dot_general(a, b, (((1,), (1,)), ((), ())), preferred_element_type=F32)


def nn(a, b):
    return lax.dot_general(a, b, (((1,), (0,)), ((), ())), preferred_element_type=F32)


def tn(a, b):
    return lax.dot_general(a, b, (((0,), (0,)), ((), ())), preferred_element_type=F32)


def fold(x, op):
    return op(x.reshape(x.shape[0] // 8, 8, x.shape[1]), axis=0)


class Pair:
    def __init__(self, scale, frames, qf, kf, st, bt, at, bh, ah, v, gr, gh, da, dv, ds, cmax, csum, cdel):
        self.__dict__.update(locals())

    def scores(self, c):
        rows = pl.ds(c * KC, KC)
        st = nt(self.kf[rows], self.qf[...]) * (self.scale * math.log2(math.e))
        self.st[rows] = st
        top = fold(st, jnp.max)
        self.cmax[...] = top if c == 0 else jnp.maximum(self.cmax[...], top)
        e = jnp.exp2(st - jnp.max(st, axis=1, keepdims=True))
        b = e * (1.0 / jnp.sum(e, axis=1, keepdims=True))
        self.bt[rows] = b
        bh = b.astype(BF16)
        self.bh[rows] = bh
        self.v[rows] = nn(bh, self.qf[...]).astype(BF16)

    def attend(self):
        top = jnp.max(self.cmax[...], axis=0, keepdims=True)
        total = jnp.zeros((8, TOK), F32)
        for c in range(TOK // KC):
            rows = pl.ds(c * KC, KC)
            e = jnp.exp2(self.st[rows] - top)
            self.at[rows] = e
            total = total + fold(e, jnp.sum)
        inv = 1.0 / jnp.sum(total, axis=0, keepdims=True)
        for c in range(TOK // KC):
            rows = pl.ds(c * KC, KC)
            a = self.at[rows] * inv
            self.at[rows] = a
            self.ah[rows] = a.astype(BF16)

    def residual(self, size=384):
        for c in range(TOK // size):
            rows = pl.ds(c * size, size)
            cycled = tn(self.ah[:, rows], self.v[...])
            g = (cycled - self.qf[rows].astype(F32)) * (1.0 / self.frames)
            self.gr[rows] = g
            self.gh[rows] = g.astype(BF16)

    def grad_rows(self, size=384):
        total = jnp.zeros((8, TOK), F32)
        for c in range(TOK // size):
            rows = pl.ds(c * size, size)
            da = nt(self.v[rows], self.gh[...])
            self.da[rows] = da
            total = total + fold(da * self.at[rows], jnp.sum)
        self.cdel[...] = jnp.broadcast_to(jnp.sum(total, axis=0, keepdims=True), (8, TOK))

    def grad_warp(self, size=384):
        for c in range(TOK // size):
            rows = pl.ds(c * size, size)
            self.dv[rows] = nn(self.ah[rows], self.gh[...]).astype(BF16)

    def grad_scores(self, c, size=KC):
        rows = pl.ds(c * size, size)
        db = nt(self.dv[rows], self.qf[...])
        b = self.bt[rows]
        delta = jnp.sum(db * b, axis=1, keepdims=True)
        ds = self.at[rows] * (self.da[rows] - self.cdel[0:1]) + b * (db - delta)
        dsh = (ds * self.scale).astype(BF16)
        self.ds[rows] = dsh
        return nn(dsh, self.qf[...])

    def query_terms(self, c, size=384):
        rows = pl.ds(c * size, size)
        return tn(self.bh[:, rows], self.dv[...]) + tn(self.ds[:, rows], self.kf[...]) - self.gr[rows]


def pair_scratch():
    def whole(dtype):
        return pltpu.VMEM((TOK, TOK), dtype)

    return [
        whole(F32), whole(F32), whole(F32), whole(BF16), whole(BF16), whole(BF16),
        whole(F32), whole(BF16), whole(F32), whole(BF16), whole(BF16),
        pltpu.VMEM((8, TOK), F32), pltpu.VMEM((8, TOK), F32), pltpu.VMEM((8, TOK), F32),
    ]


ZORDER = (0, 1, 3, 2)


def krow(dx, dz):
    return (ZORDER.index(dz % 4) * 4 + dx % 4) * ROWS


def qrow(dy, dzl, dc):
    return (((1 - dzl) * 2 + 1 - dc) * 4 + dy % 4) * ROWS


def cycle_kernel(scale, frames, q_hbm, k_hbm, q_out, k_out, qf, kf, *scratch):
    pair = Pair(scale, frames, qf, kf, *scratch[:14])
    (
        kst, kp, kx1, kx2, kzt, kzin, qcst, qcin, qp, qst, qyin, qzst, qzin,
        own_sem, send_sem, q_sem, k_sem,
        kx1_sem, kx2_sem, kzt_sem, kzin_sem, qc_sem, qy_sem, qz_sem,
    ) = scratch[14:]
    at = Place()

    def kblock(dx, dz):
        return kf.at[pl.ds(krow(dx, dz), ROWS)]

    def qblock(dy, dzl, dc):
        return qf.at[pl.ds(qrow(dy, dzl, dc), ROWS)]

    own_q = pltpu.make_async_copy(q_hbm.at[0], qblock(0, 0, 0), own_sem.at[0])
    own_k = pltpu.make_async_copy(k_hbm.at[0], kblock(0, 0), own_sem.at[1])
    own_q.start()
    own_k.start()
    greet(at)
    own_q.wait()
    own_k.wait()
    out = Sends(send_sem)

    def got(ref, sem):
        pltpu.make_async_remote_copy(
            src_ref=ref, dst_ref=ref, send_sem=send_sem.at[0],
            recv_sem=sem, device_id=at.at_core(), device_id_type=MESH,
        ).wait_recv()


    def ksem(dx, dz):
        return k_sem.at[krow(dx, dz) // ROWS]

    def qsem(dy, dzl, dc):
        return q_sem.at[qrow(dy, dzl, dc) // ROWS]

    def got_k(dx, dz):
        got(kblock(dx, dz), ksem(dx, dz))

    def got_q(dy, dzl, dc):
        got(qblock(dy, dzl, dc), qsem(dy, dzl, dc))

    def k_along_x(dz, steps):
        for step in steps:
            out.go(kblock(0, dz), kblock(-step, dz), ksem(-step, dz), at.at_x(step))

    def k_along_z(dx, steps):
        for step in steps:
            out.go(kblock(dx, 0), kblock(dx, -step), ksem(dx, -step), at.at_zh(step))

    def q_along_y(dzl):
        for step in (1, -1, 2):
            out.go(qblock(0, dzl, 0), qblock(-step, dzl, 0), qsem(-step, dzl, 0), at.at_y(step))

    def q_to_core(dy, dzl):
        out.go(qblock(dy, dzl, 0), qblock(dy, dzl, 1), qsem(dy, dzl, 1), at.at_core())

    out.go(qblock(0, 0, 0), qblock(0, 1, 0), qsem(0, 1, 0), at.at_zl())
    k_along_z(0, (1, -1))
    k_along_x(0, (1, -1))
    q_along_y(0)
    k_along_z(0, (2,))
    k_along_x(0, (2,))
    q_to_core(0, 0)

    got_q(0, 1, 0)
    q_along_y(1)
    q_to_core(0, 1)
    for dz in (1, 3):
        got_k(0, dz)
        k_along_x(dz, (1, -1))
    for dy in (1, 3, 2):
        got_q(dy, 0, 0)
        q_to_core(dy, 0)
    got_k(2, 0)
    k_along_z(2, (1, -1))
    got_k(0, 2)
    k_along_x(2, (1, -1, 2))
    for dy in (1, 3, 2):
        got_q(dy, 1, 0)
        q_to_core(dy, 1)
    for dzl in (0, 1):
        for dy in (0, 1, 3, 2):
            got_q(dy, dzl, 1)

    got_k(1, 0)
    got_k(3, 0)
    for c, dz in enumerate(ZORDER):
        if dz != 0:
            for dx in (1, 3, 2):
                got_k(dx, dz)
        pair.scores(c)
    pair.attend()
    pair.residual()
    pair.grad_rows()
    pair.grad_warp()

    def send_k(dx, dz, dst, sem, device):
        out.go(kst.at[pl.ds(krow(dx, dz), ROWS)], dst, sem, device)

    for c in (3, 1, 2, 0):
        dz = ZORDER[c]
        terms = pair.grad_scores(c)
        kst[pl.ds(c * KC, KC)] = terms.astype(BF16)
        kp[dz] = terms[0:ROWS]
        if dz == 0:
            kp[4] = terms[2 * ROWS : 3 * ROWS]
        if dz == 1:
            send_k(2, 1, kzt.at[0], kzt_sem.at[0], at.at_zh(1))
        if dz == 3:
            send_k(2, 3, kzt.at[1], kzt_sem.at[1], at.at_zh(-1))
        if dz == 2:
            send_k(2, 2, kx2.at[1], kx2_sem.at[1], at.at_x(2))
        send_k(1, dz, kx1.at[dz], kx1_sem.at[dz], at.at_x(1))
        send_k(3, dz, kx1.at[4 + dz], kx1_sem.at[4 + dz], at.at_x(-1))

    for dzl in (1, 0):
        terms = pair.query_terms(1 - dzl)
        rows = pl.ds(dzl * KC, KC)
        qcst[rows] = terms[0:KC].astype(BF16)
        qp[rows] = terms[KC : 2 * KC]
        for dy in (2, 1, 3, 0):
            slot = dzl * 4 + dy
            block = pl.ds(slot * ROWS, ROWS)
            out.go(qcst.at[block], qcin.at[block], qc_sem.at[slot], at.at_core())

    def core_sum(dy, dzl):
        slot = dzl * 4 + dy
        block = pl.ds(slot * ROWS, ROWS)
        got(qcin.at[block], qc_sem.at[slot])
        return qp[block] + qcin[block].astype(F32)

    def q_along_y_sums(dzl):
        for dy in (2, 1, 3):
            slot = dzl * 4 + dy
            qst[slot] = core_sum(dy, dzl).astype(BF16)
            out.go(qst.at[slot], qyin.at[slot], qy_sem.at[slot], at.at_y(dy if dy < 3 else -1))

    q_along_y_sums(1)
    q_along_y_sums(0)

    def k_sum(dz):
        got(kx1.at[dz], kx1_sem.at[dz])
        got(kx1.at[4 + dz], kx1_sem.at[4 + dz])
        return kp[dz] + kx1[dz].astype(F32) + kx1[4 + dz].astype(F32)

    def k_send_z(dz, total):
        kst[pl.ds(krow(0, dz), ROWS)] = total.astype(BF16)
        send_k(0, dz, kzin.at[dz], kzin_sem.at[dz], at.at_zh(dz if dz < 3 else -1))

    total = k_sum(2)
    got(kx2.at[1], kx2_sem.at[1])
    k_send_z(2, total + kx2[1].astype(F32))
    for side in (0, 1):
        got(kzt.at[side], kzt_sem.at[side])
    kst[pl.ds(krow(2, 0), ROWS)] = (kp[4] + kzt[0].astype(F32) + kzt[1].astype(F32)).astype(BF16)
    send_k(2, 0, kx2.at[0], kx2_sem.at[0], at.at_x(2))
    for dz in (1, 3):
        k_send_z(dz, k_sum(dz))

    def y_sum(dzl):
        total = core_sum(0, dzl)
        for dy in (1, 3, 2):
            slot = dzl * 4 + dy
            got(qyin.at[slot], qy_sem.at[slot])
            total = total + qyin[slot].astype(F32)
        return total

    qzst[...] = y_sum(1).astype(BF16)
    out.go(qzst, qzin, qz_sem.at[0], at.at_zl())
    q_total = y_sum(0)
    total = k_sum(0)
    got(kx2.at[0], kx2_sem.at[0])
    total = total + kx2[0].astype(F32)
    got(qzin, qz_sem.at[0])
    q_out[0] = q_total + qzin[...].astype(F32)
    for dz in (1, 3, 2):
        got(kzin.at[dz], kzin_sem.at[dz])
        total = total + kzin[dz].astype(F32)
    k_out[0] = total
    out.finish()


def local(queries, keys):
    frames = queries.shape[0] * lax.axis_size("row")
    scale = queries.shape[2] ** -0.5
    vmem = pl.BlockSpec(memory_space=pltpu.VMEM)
    hbm = pl.BlockSpec(memory_space=pltpu.MemorySpace.HBM)
    own = jax.ShapeDtypeStruct((1, ROWS, TOK), F32)

    def buf(*lead, dtype=BF16):
        return pltpu.VMEM((*lead, TOK), dtype)

    def sems(count):
        return pltpu.SemaphoreType.DMA((count,))

    return pl.pallas_call(
        functools.partial(cycle_kernel, scale, frames),
        out_shape=(own, own),
        in_specs=[hbm, hbm],
        out_specs=(vmem, vmem),
        scratch_shapes=[
            buf(TOK), buf(TOK),
            *pair_scratch(),
            buf(TOK), buf(5, ROWS, dtype=F32), buf(8, ROWS), buf(2, ROWS), buf(2, ROWS), buf(4, ROWS),
            buf(8 * ROWS), buf(8 * ROWS), buf(8 * ROWS, dtype=F32), buf(8, ROWS), buf(8, ROWS), buf(ROWS), buf(ROWS),
            sems(2), sems(60), sems(16), sems(16),
            sems(8), sems(2), sems(2), sems(4), sems(8), sems(8), sems(1),
        ],
        compiler_params=pltpu.CompilerParams(
            collective_id=0, has_side_effects=True, vmem_limit_bytes=60 * 2**20
        ),
        name="cycle_pairs",
    )(queries, keys)


def solution(mesh):
    placed = (P("row", "col", None), P("col", "row", None))
    return jax.shard_map(
        local,
        mesh=mesh,
        in_specs=placed,
        out_specs=(P("row", "col", None), P("col", "row", None)),
        check_vma=False,
    )
```

```python
import functools
import math

import jax
import jax.numpy as jnp
from jax import lax
from jax.experimental import pallas as pl
from jax.experimental.pallas import tpu as pltpu
from jax.sharding import PartitionSpec as P

MESH = pl.DeviceIdType.MESH
BF16 = jnp.bfloat16
F32 = jnp.float32


class Place:
    def __init__(self):
        row = lax.axis_index("row")
        col = lax.axis_index("col")
        self.zh, self.x = row // 4, row % 4
        self.y, self.zl, self.c = col // 4, (col // 2) % 2, col % 2
        self.row, self.col = row, col

    def at_x(self, step):
        return (self.zh * 4 + (self.x + step + 4) % 4, self.col)

    def at_zh(self, step):
        return (((self.zh + step + 4) % 4) * 4 + self.x, self.col)

    def at_y(self, step):
        return (self.row, ((self.y + step + 4) % 4) * 4 + self.zl * 2 + self.c)

    def at_zl(self):
        return (self.row, self.y * 4 + (1 - self.zl) * 2 + self.c)

    def at_core(self):
        return (self.row, self.y * 4 + self.zl * 2 + 1 - self.c)


def greet(at):
    barrier = pltpu.get_barrier_semaphore()
    others = [at.at_core(), at.at_zl()]
    for step in (1, -1, 2):
        others += [at.at_x(step), at.at_y(step), at.at_zh(step)]
    for other in others:
        pl.semaphore_signal(barrier, inc=1, device_id=other, device_id_type=MESH)
    pl.semaphore_wait(barrier, len(others))


class Sends:
    def __init__(self, send_sem):
        self.send_sem = send_sem
        self.started = []

    def go(self, src, dst, recv, device):
        copy = pltpu.make_async_remote_copy(
            src_ref=src,
            dst_ref=dst,
            send_sem=self.send_sem.at[len(self.started)],
            recv_sem=recv,
            device_id=device,
            device_id_type=MESH,
        )
        copy.start()
        self.started.append(copy)

    def finish(self):
        for copy in self.started:
            copy.wait_send()


TOK = 768
ROWS = 48
KC = 192


def nt(a, b):
    return lax.dot_general(a, b, (((1,), (1,)), ((), ())), preferred_element_type=F32)


def nn(a, b):
    return lax.dot_general(a, b, (((1,), (0,)), ((), ())), preferred_element_type=F32)


def tn(a, b):
    return lax.dot_general(a, b, (((0,), (0,)), ((), ())), preferred_element_type=F32)


def fold(x, op):
    return op(x.reshape(x.shape[0] // 8, 8, x.shape[1]), axis=0)


class Pair:
    def __init__(self, scale, frames, qf, kf, st, bt, at, bh, ah, v, gr, gh, da, dv, ds, cmax, csum, cdel):
        self.__dict__.update(locals())

    def scores(self, c):
        rows = pl.ds(c * KC, KC)
        st = nt(self.kf[rows], self.qf[...]) * (self.scale * math.log2(math.e))
        self.st[rows] = st
        top = fold(st, jnp.max)
        self.cmax[...] = top if c == 0 else jnp.maximum(self.cmax[...], top)
        e = jnp.exp2(st - jnp.max(st, axis=1, keepdims=True))
        b = e * (1.0 / jnp.sum(e, axis=1, keepdims=True))
        self.bt[rows] = b
        bh = b.astype(BF16)
        self.bh[rows] = bh
        self.v[rows] = nn(bh, self.qf[...]).astype(BF16)

    def attend(self):
        top = jnp.max(self.cmax[...], axis=0, keepdims=True)
        total = jnp.zeros((8, TOK), F32)
        for c in range(TOK // KC):
            rows = pl.ds(c * KC, KC)
            e = jnp.exp2(self.st[rows] - top)
            self.at[rows] = e
            total = total + fold(e, jnp.sum)
        inv = 1.0 / jnp.sum(total, axis=0, keepdims=True)
        for c in range(TOK // KC):
            rows = pl.ds(c * KC, KC)
            a = self.at[rows] * inv
            self.at[rows] = a
            self.ah[rows] = a.astype(BF16)

    def residual(self, size=384):
        for c in range(TOK // size):
            rows = pl.ds(c * size, size)
            cycled = tn(self.ah[:, rows], self.v[...])
            g = (cycled - self.qf[rows].astype(F32)) * (1.0 / self.frames)
            self.gr[rows] = g
            self.gh[rows] = g.astype(BF16)

    def grad_rows(self, size=384):
        total = jnp.zeros((8, TOK), F32)
        for c in range(TOK // size):
            rows = pl.ds(c * size, size)
            da = nt(self.v[rows], self.gh[...])
            self.da[rows] = da
            total = total + fold(da * self.at[rows], jnp.sum)
        self.cdel[...] = jnp.broadcast_to(jnp.sum(total, axis=0, keepdims=True), (8, TOK))

    def grad_warp(self, size=384):
        for c in range(TOK // size):
            rows = pl.ds(c * size, size)
            self.dv[rows] = nn(self.ah[rows], self.gh[...]).astype(BF16)

    def grad_scores(self, c, size=384):
        rows = pl.ds(c * size, size)
        db = nt(self.dv[rows], self.qf[...])
        b = self.bt[rows]
        delta = jnp.sum(db * b, axis=1, keepdims=True)
        ds = self.at[rows] * (self.da[rows] - self.cdel[0:1]) + b * (db - delta)
        self.ds[rows] = (ds * self.scale).astype(BF16)

    def key_terms(self, c, size=KC):
        return nn(self.ds[pl.ds(c * size, size)], self.qf[...])

    def query_terms(self, c, size=384):
        rows = pl.ds(c * size, size)
        return tn(self.bh[:, rows], self.dv[...]) + tn(self.ds[:, rows], self.kf[...]) - self.gr[rows]


def pair_scratch():
    def whole(dtype):
        return pltpu.VMEM((TOK, TOK), dtype)

    return [
        whole(F32), whole(F32), whole(F32), whole(BF16), whole(BF16), whole(BF16),
        whole(F32), whole(BF16), whole(F32), whole(BF16), whole(BF16),
        pltpu.VMEM((8, TOK), F32), pltpu.VMEM((8, TOK), F32), pltpu.VMEM((8, TOK), F32),
    ]


ZORDER = (0, 1, 3, 2)


def krow(dx, dz):
    return (ZORDER.index(dz % 4) * 4 + dx % 4) * ROWS


def qrow(dy, dzl, dc):
    return (((1 - dzl) * 2 + 1 - dc) * 4 + dy % 4) * ROWS


def cycle_kernel(scale, frames, q_hbm, k_hbm, q_out, k_out, qf, kf, *scratch):
    pair = Pair(scale, frames, qf, kf, *scratch[:14])
    (
        kst, kp, kx1, kx2, kzt, kzin, qcst, qcin, qp, qst, qyin, qzst, qzin,
        own_sem, send_sem, q_sem, k_sem,
        kx1_sem, kx2_sem, kzt_sem, kzin_sem, qc_sem, qy_sem, qz_sem,
    ) = scratch[14:]
    at = Place()

    def kblock(dx, dz):
        return kf.at[pl.ds(krow(dx, dz), ROWS)]

    def qblock(dy, dzl, dc):
        return qf.at[pl.ds(qrow(dy, dzl, dc), ROWS)]

    own_q = pltpu.make_async_copy(q_hbm.at[0], qblock(0, 0, 0), own_sem.at[0])
    own_k = pltpu.make_async_copy(k_hbm.at[0], kblock(0, 0), own_sem.at[1])
    own_q.start()
    own_k.start()
    greet(at)
    own_q.wait()
    own_k.wait()
    out = Sends(send_sem)

    def got(ref, sem):
        pltpu.make_async_remote_copy(
            src_ref=ref, dst_ref=ref, send_sem=send_sem.at[0],
            recv_sem=sem, device_id=at.at_core(), device_id_type=MESH,
        ).wait_recv()


    def ksem(dx, dz):
        return k_sem.at[krow(dx, dz) // ROWS]

    def qsem(dy, dzl, dc):
        return q_sem.at[qrow(dy, dzl, dc) // ROWS]

    def got_k(dx, dz):
        got(kblock(dx, dz), ksem(dx, dz))

    def got_q(dy, dzl, dc):
        got(qblock(dy, dzl, dc), qsem(dy, dzl, dc))

    def k_along_x(dz, steps):
        for step in steps:
            out.go(kblock(0, dz), kblock(-step, dz), ksem(-step, dz), at.at_x(step))

    def k_along_z(dx, steps):
        for step in steps:
            out.go(kblock(dx, 0), kblock(dx, -step), ksem(dx, -step), at.at_zh(step))

    def q_along_y(dzl):
        for step in (1, -1, 2):
            out.go(qblock(0, dzl, 0), qblock(-step, dzl, 0), qsem(-step, dzl, 0), at.at_y(step))

    def q_to_core(dy, dzl):
        out.go(qblock(dy, dzl, 0), qblock(dy, dzl, 1), qsem(dy, dzl, 1), at.at_core())

    out.go(qblock(0, 0, 0), qblock(0, 1, 0), qsem(0, 1, 0), at.at_zl())
    k_along_z(0, (1, -1))
    k_along_x(0, (2, 1, -1))
    q_along_y(0)
    k_along_z(0, (2,))
    q_to_core(0, 0)

    got_q(0, 1, 0)
    q_along_y(1)
    q_to_core(0, 1)
    for dz in (1, 3):
        got_k(0, dz)
        k_along_x(dz, (1, -1))
    for dy in (1, 3, 2):
        got_q(dy, 0, 0)
        q_to_core(dy, 0)
    got_k(2, 0)
    k_along_z(2, (1, -1))
    got_k(0, 2)
    k_along_x(2, (2, 1, -1))
    for dy in (1, 3, 2):
        got_q(dy, 1, 0)
        q_to_core(dy, 1)
    for dzl in (0, 1):
        for dy in (0, 1, 3, 2):
            got_q(dy, dzl, 1)

    got_k(1, 0)
    got_k(3, 0)
    for c, dz in enumerate(ZORDER):
        if dz != 0:
            for dx in (1, 3, 2):
                got_k(dx, dz)
        pair.scores(c)
    pair.attend()
    pair.residual()
    pair.grad_rows()
    pair.grad_warp()

    def send_k(dx, dz, dst, sem, device):
        out.go(kst.at[pl.ds(krow(dx, dz), ROWS)], dst, sem, device)

    for c in (3, 2, 1, 0):
        dz = ZORDER[c]
        if c % 2 == 1:
            pair.grad_scores(c // 2)
        terms = pair.key_terms(c)
        kst[pl.ds(c * KC, KC)] = terms.astype(BF16)
        kp[dz] = terms[0:ROWS]
        if dz == 0:
            kp[4] = terms[2 * ROWS : 3 * ROWS]
        if dz == 1:
            send_k(2, 1, kzt.at[0], kzt_sem.at[0], at.at_zh(1))
        if dz == 3:
            send_k(2, 3, kzt.at[1], kzt_sem.at[1], at.at_zh(-1))
        if dz == 2:
            send_k(2, 2, kx2.at[1], kx2_sem.at[1], at.at_x(2))
        send_k(1, dz, kx1.at[dz], kx1_sem.at[dz], at.at_x(1))
        send_k(3, dz, kx1.at[4 + dz], kx1_sem.at[4 + dz], at.at_x(-1))

    for dzl in (1, 0):
        terms = pair.query_terms(1 - dzl)
        rows = pl.ds(dzl * KC, KC)
        qcst[rows] = terms[0:KC].astype(BF16)
        qp[rows] = terms[KC : 2 * KC]
        for dy in (2, 1, 3, 0):
            slot = dzl * 4 + dy
            block = pl.ds(slot * ROWS, ROWS)
            out.go(qcst.at[block], qcin.at[block], qc_sem.at[slot], at.at_core())

    def core_sum(dy, dzl):
        slot = dzl * 4 + dy
        block = pl.ds(slot * ROWS, ROWS)
        got(qcin.at[block], qc_sem.at[slot])
        return qp[block] + qcin[block].astype(F32)

    def q_along_y_sums(dzl):
        for dy in (2, 1, 3):
            slot = dzl * 4 + dy
            qst[slot] = core_sum(dy, dzl).astype(BF16)
            out.go(qst.at[slot], qyin.at[slot], qy_sem.at[slot], at.at_y(dy if dy < 3 else -1))

    def k_sum(dz):
        got(kx1.at[dz], kx1_sem.at[dz])
        got(kx1.at[4 + dz], kx1_sem.at[4 + dz])
        return kp[dz] + kx1[dz].astype(F32) + kx1[4 + dz].astype(F32)

    def k_send_z(dz, total):
        kst[pl.ds(krow(0, dz), ROWS)] = total.astype(BF16)
        send_k(0, dz, kzin.at[dz], kzin_sem.at[dz], at.at_zh(dz if dz < 3 else -1))

    q_along_y_sums(1)
    total = k_sum(2)
    got(kx2.at[1], kx2_sem.at[1])
    k_send_z(2, total + kx2[1].astype(F32))
    q_along_y_sums(0)
    for side in (0, 1):
        got(kzt.at[side], kzt_sem.at[side])
    kst[pl.ds(krow(2, 0), ROWS)] = (kp[4] + kzt[0].astype(F32) + kzt[1].astype(F32)).astype(BF16)
    send_k(2, 0, kx2.at[0], kx2_sem.at[0], at.at_x(2))
    for dz in (1, 3):
        k_send_z(dz, k_sum(dz))

    def y_sum(dzl):
        total = core_sum(0, dzl)
        for dy in (1, 3, 2):
            slot = dzl * 4 + dy
            got(qyin.at[slot], qy_sem.at[slot])
            total = total + qyin[slot].astype(F32)
        return total

    qzst[...] = y_sum(1).astype(BF16)
    out.go(qzst, qzin, qz_sem.at[0], at.at_zl())
    q_total = y_sum(0)
    total = k_sum(0)
    got(kx2.at[0], kx2_sem.at[0])
    total = total + kx2[0].astype(F32)
    got(qzin, qz_sem.at[0])
    q_out[0] = q_total + qzin[...].astype(F32)
    for dz in (1, 3, 2):
        got(kzin.at[dz], kzin_sem.at[dz])
        total = total + kzin[dz].astype(F32)
    k_out[0] = total
    out.finish()


def local(queries, keys):
    frames = queries.shape[0] * lax.axis_size("row")
    scale = queries.shape[2] ** -0.5
    vmem = pl.BlockSpec(memory_space=pltpu.VMEM)
    hbm = pl.BlockSpec(memory_space=pltpu.MemorySpace.HBM)
    own = jax.ShapeDtypeStruct((1, ROWS, TOK), F32)

    def buf(*lead, dtype=BF16):
        return pltpu.VMEM((*lead, TOK), dtype)

    def sems(count):
        return pltpu.SemaphoreType.DMA((count,))

    return pl.pallas_call(
        functools.partial(cycle_kernel, scale, frames),
        out_shape=(own, own),
        in_specs=[hbm, hbm],
        out_specs=(vmem, vmem),
        scratch_shapes=[
            buf(TOK), buf(TOK),
            *pair_scratch(),
            buf(TOK), buf(5, ROWS, dtype=F32), buf(8, ROWS), buf(2, ROWS), buf(2, ROWS), buf(4, ROWS),
            buf(8 * ROWS), buf(8 * ROWS), buf(8 * ROWS, dtype=F32), buf(8, ROWS), buf(8, ROWS), buf(ROWS), buf(ROWS),
            sems(2), sems(60), sems(16), sems(16),
            sems(8), sems(2), sems(2), sems(4), sems(8), sems(8), sems(1),
        ],
        compiler_params=pltpu.CompilerParams(
            collective_id=0, has_side_effects=True, vmem_limit_bytes=44 * 2**20
        ),
        name="cycle_pairs",
    )(
        pltpu.with_memory_space_constraint(queries, pltpu.HBM),
        pltpu.with_memory_space_constraint(keys, pltpu.HBM),
    )


def solution(mesh):
    placed = (P("row", "col", None), P("col", "row", None))
    return jax.shard_map(
        local,
        mesh=mesh,
        in_specs=placed,
        out_specs=(P("row", "col", None), P("col", "row", None)),
        check_vma=False,
    )
```

```python
import functools
import math

import jax
import jax.numpy as jnp
from jax import lax
from jax.experimental import pallas as pl
from jax.experimental.pallas import tpu as pltpu
from jax.sharding import PartitionSpec as P

MESH = pl.DeviceIdType.MESH
BF16 = jnp.bfloat16
F32 = jnp.float32


class Place:
    def __init__(self):
        row = lax.axis_index("row")
        col = lax.axis_index("col")
        self.zh, self.x = row // 4, row % 4
        self.y, self.zl, self.c = col // 4, (col // 2) % 2, col % 2
        self.row, self.col = row, col

    def at_x(self, step):
        return (self.zh * 4 + (self.x + step + 4) % 4, self.col)

    def at_zh(self, step):
        return (((self.zh + step + 4) % 4) * 4 + self.x, self.col)

    def at_y(self, step):
        return (self.row, ((self.y + step + 4) % 4) * 4 + self.zl * 2 + self.c)

    def at_zl(self):
        return (self.row, self.y * 4 + (1 - self.zl) * 2 + self.c)

    def at_core(self):
        return (self.row, self.y * 4 + self.zl * 2 + 1 - self.c)


def greet(at):
    barrier = pltpu.get_barrier_semaphore()
    others = [at.at_core(), at.at_zl()]
    for step in (1, -1, 2):
        others += [at.at_x(step), at.at_y(step), at.at_zh(step)]
    for other in others:
        pl.semaphore_signal(barrier, inc=1, device_id=other, device_id_type=MESH)
    pl.semaphore_wait(barrier, len(others))


class Sends:
    def __init__(self, send_sem):
        self.send_sem = send_sem
        self.started = []

    def go(self, src, dst, recv, device):
        copy = pltpu.make_async_remote_copy(
            src_ref=src,
            dst_ref=dst,
            send_sem=self.send_sem.at[len(self.started)],
            recv_sem=recv,
            device_id=device,
            device_id_type=MESH,
        )
        copy.start()
        self.started.append(copy)

    def finish(self):
        for copy in self.started:
            copy.wait_send()


TOK = 768
ROWS = 48
KC = 192


def nt(a, b):
    return lax.dot_general(a, b, (((1,), (1,)), ((), ())), preferred_element_type=F32)


def nn(a, b):
    return lax.dot_general(a, b, (((1,), (0,)), ((), ())), preferred_element_type=F32)


def tn(a, b):
    return lax.dot_general(a, b, (((0,), (0,)), ((), ())), preferred_element_type=F32)


def fold(x, op):
    return op(x.reshape(x.shape[0] // 8, 8, x.shape[1]), axis=0)


class Pair:
    def __init__(self, scale, frames, qf, kf, st, bt, at, bh, ah, v, gr, gh, dv, ds, cmax, etop, csum, cdel):
        self.__dict__.update(locals())

    def scores(self, start, size):
        rows = pl.ds(start, size)
        st = nt(self.kf[rows], self.qf[...]) * (self.scale * math.log2(math.e))
        self.st[rows] = st
        top = fold(st, jnp.max)
        self.cmax[...] = top if start == 0 else jnp.maximum(self.cmax[...], top)
        e = jnp.exp2(st - jnp.max(st, axis=1, keepdims=True))
        b = e * (1.0 / jnp.sum(e, axis=1, keepdims=True))
        self.bt[rows] = b
        bh = b.astype(BF16)
        self.bh[rows] = bh
        self.v[rows] = nn(bh, self.qf[...]).astype(BF16)

    def powers(self, start, size, top):
        total = jnp.zeros((8, TOK), F32)
        for first in range(start, start + size, KC):
            rows = pl.ds(first, KC)
            e = jnp.exp2(self.st[rows] - top)
            self.at[rows] = e
            total = total + fold(e, jnp.sum)
        return total

    def attend_early(self, size):
        top = jnp.max(self.cmax[...], axis=0, keepdims=True)
        self.etop[...] = jnp.broadcast_to(top, (8, TOK))
        self.csum[...] = self.powers(0, size, top)

    def attend(self, size):
        top = jnp.max(self.cmax[...], axis=0, keepdims=True)
        early = jnp.exp2(self.etop[0:1] - top)
        late = self.powers(size, TOK - size, top)
        total = jnp.sum(self.csum[...] * early + late, axis=0, keepdims=True)
        inv = 1.0 / total
        weight = early * inv
        halves = jnp.zeros((8, TOK), F32)
        for first in range(0, TOK, KC):
            rows = pl.ds(first, KC)
            a = self.at[rows] * (weight if first < size else inv)
            self.at[rows] = a
            ah = a.astype(BF16)
            self.ah[rows] = ah
            halves = halves + fold(ah.astype(F32), jnp.sum)
        self.csum[...] = jnp.broadcast_to(jnp.sum(halves, axis=0, keepdims=True), (8, TOK))

    def residual(self, size=384):
        for c in range(TOK // size):
            rows = pl.ds(c * size, size)
            cycled = tn(self.ah[:, rows], self.v[...])
            g = (cycled - self.qf[rows].astype(F32)) * (1.0 / self.frames)
            gh = g.astype(BF16)
            self.gr[rows] = g
            self.gh[rows] = gh
            delta = jnp.sum(gh.astype(F32) * cycled, axis=1, keepdims=True)
            self.cdel[:, rows] = jnp.broadcast_to(delta, (size, 128)).T[0:8] / self.csum[:, rows]

    def grad_scores(self, start, size):
        rows = pl.ds(start, size)
        da = nt(self.v[rows], self.gh[...])
        dv = nn(self.ah[rows], self.gh[...]).astype(BF16)
        self.dv[rows] = dv
        db = nt(dv, self.qf[...])
        b = self.bt[rows]
        delta = jnp.sum(db * b, axis=1, keepdims=True)
        ds = self.at[rows] * (da - self.cdel[0:1]) + b * (db - delta)
        self.ds[rows] = (ds * self.scale).astype(BF16)

    def key_terms(self, c, size=KC):
        return nn(self.ds[pl.ds(c * size, size)], self.qf[...])

    def query_terms(self, c, size=384):
        rows = pl.ds(c * size, size)
        return tn(self.bh[:, rows], self.dv[...]) + tn(self.ds[:, rows], self.kf[...]) - self.gr[rows]


def pair_scratch():
    def whole(dtype):
        return pltpu.VMEM((TOK, TOK), dtype)

    return [
        whole(F32), whole(F32), whole(F32), whole(BF16), whole(BF16), whole(BF16),
        whole(F32), whole(BF16), whole(BF16), whole(BF16),
        *[pltpu.VMEM((8, TOK), F32)] * 4,
    ]


ZORDER = (0, 1, 3, 2)


def krow(dx, dz):
    return (ZORDER.index(dz % 4) * 4 + dx % 4) * ROWS


def qrow(dy, dzl, dc):
    return (((1 - dzl) * 2 + 1 - dc) * 4 + dy % 4) * ROWS


def cycle_kernel(scale, frames, q_hbm, k_hbm, both, qf, kf, *scratch):
    pair = Pair(scale, frames, qf, kf, *scratch[:14])
    (
        kst, kp, kx1, kx2, kzt, kzin, qcst, qcin, qp, qst, qyin, qzst, qzin,
        own_sem, send_sem, q_sem, k_sem,
        kx1_sem, kx2_sem, kzt_sem, kzin_sem, qc_sem, qy_sem, qz_sem,
    ) = scratch[14:]
    at = Place()

    def kblock(dx, dz):
        return kf.at[pl.ds(krow(dx, dz), ROWS)]

    def qblock(dy, dzl, dc):
        return qf.at[pl.ds(qrow(dy, dzl, dc), ROWS)]

    own_q = pltpu.make_async_copy(q_hbm.at[0], qblock(0, 0, 0), own_sem.at[0])
    own_k = pltpu.make_async_copy(k_hbm.at[0], kblock(0, 0), own_sem.at[1])
    own_q.start()
    own_k.start()
    greet(at)
    own_q.wait()
    own_k.wait()
    out = Sends(send_sem)

    def got(ref, sem):
        pltpu.make_async_remote_copy(
            src_ref=ref, dst_ref=ref, send_sem=send_sem.at[0],
            recv_sem=sem, device_id=at.at_core(), device_id_type=MESH,
        ).wait_recv()


    def ksem(dx, dz):
        return k_sem.at[krow(dx, dz) // ROWS]

    def qsem(dy, dzl, dc):
        return q_sem.at[qrow(dy, dzl, dc) // ROWS]

    def got_k(dx, dz):
        got(kblock(dx, dz), ksem(dx, dz))

    def got_q(dy, dzl, dc):
        got(qblock(dy, dzl, dc), qsem(dy, dzl, dc))

    def k_along_x(dz, steps):
        for step in steps:
            out.go(kblock(0, dz), kblock(-step, dz), ksem(-step, dz), at.at_x(step))

    def k_along_z(dx, steps):
        for step in steps:
            out.go(kblock(dx, 0), kblock(dx, -step), ksem(dx, -step), at.at_zh(step))

    def q_along_y(dzl):
        for step in (1, -1, 2):
            out.go(qblock(0, dzl, 0), qblock(-step, dzl, 0), qsem(-step, dzl, 0), at.at_y(step))

    def q_to_core(dy, dzl):
        out.go(qblock(dy, dzl, 0), qblock(dy, dzl, 1), qsem(dy, dzl, 1), at.at_core())

    out.go(qblock(0, 0, 0), qblock(0, 1, 0), qsem(0, 1, 0), at.at_zl())
    k_along_z(0, (1, -1))
    k_along_x(0, (2, 1, -1))
    q_along_y(0)
    k_along_z(0, (2,))
    q_to_core(0, 0)

    got_q(0, 1, 0)
    q_along_y(1)
    q_to_core(0, 1)
    for dy in (1, 3):
        got_q(dy, 0, 0)
        q_to_core(dy, 0)
    got_k(2, 0)
    k_along_z(2, (1, -1))
    got_q(2, 0, 0)
    q_to_core(2, 0)
    for dz in (1, 3):
        got_k(0, dz)
        k_along_x(dz, (1, -1))
    for dy in (1, 3, 2):
        got_q(dy, 1, 0)
        q_to_core(dy, 1)
    got_k(0, 2)
    k_along_x(2, (2, 1, -1))
    for dzl in (0, 1):
        for dy in (0, 1, 3, 2):
            got_q(dy, dzl, 1)

    got_k(1, 0)
    got_k(3, 0)
    pair.scores(0, KC)
    for dz in (1, 3):
        for dx in (1, 3, 2):
            got_k(dx, dz)
    pair.scores(KC, 2 * KC)
    pair.attend_early(3 * KC)
    for dx in (1, 3, 2):
        got_k(dx, 2)
    pair.scores(3 * KC, KC)
    pair.attend(3 * KC)
    pair.residual()

    def send_k(dx, dz, dst, sem, device):
        out.go(kst.at[pl.ds(krow(dx, dz), ROWS)], dst, sem, device)

    def key_terms(dz):
        c = ZORDER.index(dz)
        terms = pair.key_terms(c)
        kst[pl.ds(c * KC, KC)] = terms.astype(BF16)
        kp[dz] = terms[0:ROWS]
        if dz == 0:
            kp[4] = terms[2 * ROWS : 3 * ROWS]
        if dz == 1:
            send_k(2, 1, kzt.at[0], kzt_sem.at[0], at.at_zh(1))
        if dz == 3:
            send_k(2, 3, kzt.at[1], kzt_sem.at[1], at.at_zh(-1))
        if dz == 2:
            send_k(2, 2, kx2.at[1], kx2_sem.at[1], at.at_x(2))
        send_k(1, dz, kx1.at[dz], kx1_sem.at[dz], at.at_x(1))
        send_k(3, dz, kx1.at[4 + dz], kx1_sem.at[4 + dz], at.at_x(-1))

    def query_terms(dzl):
        terms = pair.query_terms(1 - dzl)
        rows = pl.ds(dzl * KC, KC)
        qcst[rows] = terms[0:KC].astype(BF16)
        qp[rows] = terms[KC : 2 * KC]
        for dy in (2, 1, 3, 0):
            slot = dzl * 4 + dy
            block = pl.ds(slot * ROWS, ROWS)
            out.go(qcst.at[block], qcin.at[block], qc_sem.at[slot], at.at_core())

    pair.grad_scores(3 * KC, KC)
    key_terms(2)
    pair.grad_scores(0, 3 * KC)
    key_terms(1)
    key_terms(3)
    query_terms(1)
    key_terms(0)
    query_terms(0)

    def core_sum(dy, dzl):
        slot = dzl * 4 + dy
        block = pl.ds(slot * ROWS, ROWS)
        got(qcin.at[block], qc_sem.at[slot])
        return qp[block] + qcin[block].astype(F32)

    def q_along_y_sums(dzl):
        for dy in (2, 1, 3):
            slot = dzl * 4 + dy
            qst[slot] = core_sum(dy, dzl).astype(BF16)
            out.go(qst.at[slot], qyin.at[slot], qy_sem.at[slot], at.at_y(dy if dy < 3 else -1))

    def k_sum(dz):
        got(kx1.at[dz], kx1_sem.at[dz])
        got(kx1.at[4 + dz], kx1_sem.at[4 + dz])
        return kp[dz] + kx1[dz].astype(F32) + kx1[4 + dz].astype(F32)

    def k_send_z(dz, total):
        kst[pl.ds(krow(0, dz), ROWS)] = total.astype(BF16)
        send_k(0, dz, kzin.at[dz], kzin_sem.at[dz], at.at_zh(dz if dz < 3 else -1))

    total = k_sum(2)
    got(kx2.at[1], kx2_sem.at[1])
    k_send_z(2, total + kx2[1].astype(F32))
    q_along_y_sums(1)
    k_send_z(3, k_sum(3))
    q_along_y_sums(0)
    k_send_z(1, k_sum(1))
    for side in (0, 1):
        got(kzt.at[side], kzt_sem.at[side])
    kst[pl.ds(krow(2, 0), ROWS)] = (kp[4] + kzt[0].astype(F32) + kzt[1].astype(F32)).astype(BF16)
    send_k(2, 0, kx2.at[0], kx2_sem.at[0], at.at_x(2))

    def y_sum(dzl):
        total = core_sum(0, dzl)
        for dy in (1, 3, 2):
            slot = dzl * 4 + dy
            got(qyin.at[slot], qy_sem.at[slot])
            total = total + qyin[slot].astype(F32)
        return total

    qzst[...] = y_sum(1).astype(BF16)
    out.go(qzst, qzin, qz_sem.at[0], at.at_zl())
    q_total = y_sum(0)
    total = k_sum(0)
    got(kx2.at[0], kx2_sem.at[0])
    total = total + kx2[0].astype(F32)
    got(qzin, qz_sem.at[0])
    both[0] = q_total + qzin[...].astype(F32)
    for dz in (1, 3, 2):
        got(kzin.at[dz], kzin_sem.at[dz])
        total = total + kzin[dz].astype(F32)
    both[1] = total
    out.finish()


def local(queries, keys):
    frames = queries.shape[0] * lax.axis_size("row")
    scale = queries.shape[2] ** -0.5
    vmem = pl.BlockSpec(memory_space=pltpu.VMEM)
    hbm = pl.BlockSpec(memory_space=pltpu.MemorySpace.HBM)
    own = jax.ShapeDtypeStruct((1, ROWS, TOK), F32)

    def buf(*lead, dtype=BF16):
        return pltpu.VMEM((*lead, TOK), dtype)

    def sems(count):
        return pltpu.SemaphoreType.DMA((count,))

    both = pl.pallas_call(
        functools.partial(cycle_kernel, scale, frames),
        out_shape=jax.ShapeDtypeStruct((2, ROWS, TOK), F32),
        in_specs=[hbm, hbm],
        out_specs=vmem,
        scratch_shapes=[
            buf(TOK), buf(TOK),
            *pair_scratch(),
            buf(TOK), buf(5, ROWS, dtype=F32), buf(8, ROWS), buf(2, ROWS), buf(2, ROWS), buf(4, ROWS),
            buf(8 * ROWS), buf(8 * ROWS), buf(8 * ROWS, dtype=F32), buf(8, ROWS), buf(8, ROWS), buf(ROWS), buf(ROWS),
            sems(2), sems(60), sems(16), sems(16),
            sems(8), sems(2), sems(2), sems(4), sems(8), sems(8), sems(1),
        ],
        compiler_params=pltpu.CompilerParams(
            collective_id=0, has_side_effects=True, vmem_limit_bytes=44 * 2**20
        ),
        name="cycle_pairs",
    )(
        pltpu.with_memory_space_constraint(queries, pltpu.HBM),
        pltpu.with_memory_space_constraint(keys, pltpu.HBM),
    )
    return (both[0:1], both[1:2])


def solution(mesh):
    placed = (P("row", "col", None), P("col", "row", None))
    return jax.shard_map(
        local,
        mesh=mesh,
        in_specs=placed,
        out_specs=(P("row", "col", None), P("col", "row", None)),
        check_vma=False,
    )
```

```python
import functools
import math

import jax
import jax.numpy as jnp
from jax import lax
from jax.experimental import pallas as pl
from jax.experimental.pallas import tpu as pltpu
from jax.sharding import PartitionSpec as P

MESH = pl.DeviceIdType.MESH
BF16 = jnp.bfloat16
F32 = jnp.float32


class Place:
    def __init__(self):
        row = lax.axis_index("row")
        col = lax.axis_index("col")
        self.zh, self.x = row // 4, row % 4
        self.y, self.zl, self.c = col // 4, (col // 2) % 2, col % 2
        self.row, self.col = row, col

    def at_x(self, step):
        return (self.zh * 4 + (self.x + step + 4) % 4, self.col)

    def at_zh(self, step):
        return (((self.zh + step + 4) % 4) * 4 + self.x, self.col)

    def at_y(self, step):
        return (self.row, ((self.y + step + 4) % 4) * 4 + self.zl * 2 + self.c)

    def at_zl(self):
        return (self.row, self.y * 4 + (1 - self.zl) * 2 + self.c)

    def at_core(self):
        return (self.row, self.y * 4 + self.zl * 2 + 1 - self.c)


def greet(at):
    barrier = pltpu.get_barrier_semaphore()
    others = [at.at_core(), at.at_zl()]
    for step in (1, -1, 2):
        others += [at.at_x(step), at.at_y(step), at.at_zh(step)]
    for other in others:
        pl.semaphore_signal(barrier, inc=1, device_id=other, device_id_type=MESH)
    pl.semaphore_wait(barrier, len(others))


class Sends:
    def __init__(self, send_sem):
        self.send_sem = send_sem
        self.started = []

    def go(self, src, dst, recv, device):
        copy = pltpu.make_async_remote_copy(
            src_ref=src,
            dst_ref=dst,
            send_sem=self.send_sem.at[len(self.started)],
            recv_sem=recv,
            device_id=device,
            device_id_type=MESH,
        )
        copy.start()
        self.started.append(copy)

    def finish(self):
        for copy in self.started:
            copy.wait_send()


TOK = 768
ROWS = 48
KC = 192


def nt(a, b):
    return lax.dot_general(a, b, (((1,), (1,)), ((), ())), preferred_element_type=F32)


def nn(a, b):
    return lax.dot_general(a, b, (((1,), (0,)), ((), ())), preferred_element_type=F32)


def tn(a, b):
    return lax.dot_general(a, b, (((0,), (0,)), ((), ())), preferred_element_type=F32)


def fold(x, op):
    return op(x.reshape(x.shape[0] // 8, 8, x.shape[1]), axis=0)


class Pair:
    def __init__(self, scale, frames, qf, kf, st, bt, at, bh, ah, v, gr, gh, dv, ds, cmax, etop, csum, cdel):
        self.__dict__.update(locals())

    def scores(self, start, size):
        rows = pl.ds(start, size)
        st = nt(self.kf[rows], self.qf[...]) * (self.scale * math.log2(math.e))
        self.st[rows] = st
        top = fold(st, jnp.max)
        self.cmax[...] = top if start == 0 else jnp.maximum(self.cmax[...], top)
        e = jnp.exp2(st - jnp.max(st, axis=1, keepdims=True))
        b = e * (1.0 / jnp.sum(e, axis=1, keepdims=True))
        self.bt[rows] = b
        bh = b.astype(BF16)
        self.bh[rows] = bh
        self.v[rows] = nn(bh, self.qf[...]).astype(BF16)

    def powers(self, start, size, top):
        total = jnp.zeros((8, TOK), F32)
        for first in range(start, start + size, KC):
            rows = pl.ds(first, KC)
            e = jnp.exp2(self.st[rows] - top)
            self.at[rows] = e
            total = total + fold(e, jnp.sum)
        return total

    def attend_early(self, size):
        top = jnp.max(self.cmax[...], axis=0, keepdims=True)
        self.etop[...] = jnp.broadcast_to(top, (8, TOK))
        self.csum[...] = self.powers(0, size, top)

    def attend(self, size):
        top = jnp.max(self.cmax[...], axis=0, keepdims=True)
        early = jnp.exp2(self.etop[0:1] - top)
        late = self.powers(size, TOK - size, top)
        total = jnp.sum(self.csum[...] * early + late, axis=0, keepdims=True)
        inv = 1.0 / total
        weight = early * inv
        halves = jnp.zeros((8, TOK), F32)
        for first in range(0, TOK, KC):
            rows = pl.ds(first, KC)
            a = self.at[rows] * (weight if first < size else inv)
            self.at[rows] = a
            ah = a.astype(BF16)
            self.ah[rows] = ah
            halves = halves + fold(ah.astype(F32), jnp.sum)
        self.csum[...] = jnp.broadcast_to(jnp.sum(halves, axis=0, keepdims=True), (8, TOK))

    def residual(self, size=384):
        for c in range(TOK // size):
            rows = pl.ds(c * size, size)
            cycled = tn(self.ah[:, rows], self.v[...])
            g = (cycled - self.qf[rows].astype(F32)) * (1.0 / self.frames)
            gh = g.astype(BF16)
            self.gr[rows] = g
            self.gh[rows] = gh
            delta = jnp.sum(gh.astype(F32) * cycled, axis=1, keepdims=True)
            self.cdel[:, rows] = jnp.broadcast_to(delta, (size, 128)).T[0:8] / self.csum[:, rows]

    def grad_scores(self, start, size):
        rows = pl.ds(start, size)
        da = nt(self.v[rows], self.gh[...])
        dv = nn(self.ah[rows], self.gh[...]).astype(BF16)
        self.dv[rows] = dv
        db = nt(dv, self.qf[...])
        b = self.bt[rows]
        delta = jnp.sum(db * b, axis=1, keepdims=True)
        ds = self.at[rows] * (da - self.cdel[0:1]) + b * (db - delta)
        self.ds[rows] = (ds * self.scale).astype(BF16)

    def key_terms(self, c, size=KC):
        return nn(self.ds[pl.ds(c * size, size)], self.qf[...])

    def query_terms(self, c, size=384):
        rows = pl.ds(c * size, size)
        return tn(self.bh[:, rows], self.dv[...]) + tn(self.ds[:, rows], self.kf[...]) - self.gr[rows]


def pair_scratch():
    def whole(dtype):
        return pltpu.VMEM((TOK, TOK), dtype)

    return [
        whole(F32), whole(F32), whole(F32), whole(BF16), whole(BF16), whole(BF16),
        whole(F32), whole(BF16), whole(BF16), whole(BF16),
        *[pltpu.VMEM((8, TOK), F32)] * 4,
    ]


ZORDER = (0, 1, 3, 2)


PIECES = ((0, 32), (32, 16))


def krow(dx, dz):
    return (ZORDER.index(dz % 4) * 4 + dx % 4) * ROWS


def qrow(dy, dzl, dc):
    return (((1 - dzl) * 2 + 1 - dc) * 4 + dy % 4) * ROWS


def cycle_kernel(scale, frames, q_hbm, k_hbm, both, qf, kf, *scratch):
    pair = Pair(scale, frames, qf, kf, *scratch[:14])
    (
        kst, kp, kx1, kx2, kzt, kzin, qcst, qcin, qp, qst, qyin, qzst, qzin,
        own_sem, send_sem, q_sem, k_sem,
        kx1_sem, kx2_sem, kzt_sem, kzin_sem, qc_sem, qy_sem, qz_sem,
    ) = scratch[14:]
    at = Place()

    def kblock(dx, dz):
        return kf.at[pl.ds(krow(dx, dz), ROWS)]

    def qblock(dy, dzl, dc):
        return qf.at[pl.ds(qrow(dy, dzl, dc), ROWS)]

    own_q = pltpu.make_async_copy(q_hbm.at[0], qblock(0, 0, 0), own_sem.at[0])
    own_k = pltpu.make_async_copy(k_hbm.at[0], kblock(0, 0), own_sem.at[1])
    own_q.start()
    own_k.start()
    greet(at)
    own_q.wait()
    own_k.wait()
    out = Sends(send_sem)

    def got(ref, sem):
        pltpu.make_async_remote_copy(
            src_ref=ref, dst_ref=ref, send_sem=send_sem.at[0],
            recv_sem=sem, device_id=at.at_core(), device_id_type=MESH,
        ).wait_recv()


    def ksem(dx, dz):
        return k_sem.at[krow(dx, dz) // ROWS]

    def qsem(dy, dzl, dc):
        return q_sem.at[qrow(dy, dzl, dc) // ROWS]

    def got_k(dx, dz):
        got(kblock(dx, dz), ksem(dx, dz))

    def got_q(dy, dzl, dc):
        got(qblock(dy, dzl, dc), qsem(dy, dzl, dc))

    def k_along_x(dz, steps):
        for step in steps:
            out.go(kblock(0, dz), kblock(-step, dz), ksem(-step, dz), at.at_x(step))

    def k_along_z(dx, steps):
        for step in steps:
            out.go(kblock(dx, 0), kblock(dx, -step), ksem(dx, -step), at.at_zh(step))

    def q_along_y(dzl):
        for step in (1, -1, 2):
            out.go(qblock(0, dzl, 0), qblock(-step, dzl, 0), qsem(-step, dzl, 0), at.at_y(step))

    def q_to_core(dy, dzl):
        out.go(qblock(dy, dzl, 0), qblock(dy, dzl, 1), qsem(dy, dzl, 1), at.at_core())

    out.go(qblock(0, 0, 0), qblock(0, 1, 0), qsem(0, 1, 0), at.at_zl())
    k_along_z(0, (1, -1))
    k_along_x(0, (2, 1, -1))
    q_along_y(0)
    k_along_z(0, (2,))
    q_to_core(0, 0)

    got_q(0, 1, 0)
    q_along_y(1)
    q_to_core(0, 1)
    for dy in (1, 3):
        got_q(dy, 0, 0)
        q_to_core(dy, 0)
    got_k(2, 0)
    k_along_z(2, (1, -1))
    got_q(2, 0, 0)
    q_to_core(2, 0)
    for dz in (1, 3):
        got_k(0, dz)
        k_along_x(dz, (1, -1))
    for dy in (1, 3, 2):
        got_q(dy, 1, 0)
        q_to_core(dy, 1)
    got_k(0, 2)
    k_along_x(2, (2, 1, -1))
    for dzl in (0, 1):
        for dy in (0, 1, 3, 2):
            got_q(dy, dzl, 1)

    got_k(1, 0)
    got_k(3, 0)
    pair.scores(0, KC)
    for dz in (1, 3):
        for dx in (1, 3, 2):
            got_k(dx, dz)
    pair.scores(KC, 2 * KC)
    pair.attend_early(3 * KC)
    for dx in (1, 3, 2):
        got_k(dx, 2)
    pair.scores(3 * KC, KC)
    pair.attend(3 * KC)
    pair.residual()

    def send_k(dx, dz, dst, sem, device):
        out.go(kst.at[pl.ds(krow(dx, dz), ROWS)], dst, sem, device)

    def key_terms(dz):
        c = ZORDER.index(dz)
        terms = pair.key_terms(c)
        kst[pl.ds(c * KC, KC)] = terms.astype(BF16)
        kp[dz] = terms[0:ROWS]
        if dz == 0:
            kp[4] = terms[2 * ROWS : 3 * ROWS]
        if dz == 1:
            send_k(2, 1, kzt.at[0], kzt_sem.at[0], at.at_zh(1))
        if dz == 3:
            send_k(2, 3, kzt.at[1], kzt_sem.at[1], at.at_zh(-1))
        if dz == 2:
            for part, (first, count) in enumerate(PIECES):
                rows = pl.ds(first, count)
                for dx, dst, sem, device in (
                    (2, kx2.at[1, rows], kx2_sem.at[1 + part], at.at_x(2)),
                    (1, kx1.at[2, rows], kx1_sem.at[2 + 6 * part], at.at_x(1)),
                    (3, kx1.at[6, rows], kx1_sem.at[6 + 3 * part], at.at_x(-1)),
                ):
                    out.go(kst.at[pl.ds(krow(dx, 2) + first, count)], dst, sem, device)
            return
        send_k(1, dz, kx1.at[dz], kx1_sem.at[dz], at.at_x(1))
        send_k(3, dz, kx1.at[4 + dz], kx1_sem.at[4 + dz], at.at_x(-1))

    def query_terms(dzl):
        terms = pair.query_terms(1 - dzl)
        rows = pl.ds(dzl * KC, KC)
        qcst[rows] = terms[0:KC].astype(BF16)
        qp[rows] = terms[KC : 2 * KC]
        for dy in (2, 1, 3, 0):
            slot = dzl * 4 + dy
            block = pl.ds(slot * ROWS, ROWS)
            out.go(qcst.at[block], qcin.at[block], qc_sem.at[slot], at.at_core())

    pair.grad_scores(3 * KC, KC)
    key_terms(2)
    pair.grad_scores(0, 3 * KC)
    key_terms(1)
    key_terms(3)
    query_terms(1)
    key_terms(0)
    query_terms(0)

    def core_sum(dy, dzl):
        slot = dzl * 4 + dy
        block = pl.ds(slot * ROWS, ROWS)
        got(qcin.at[block], qc_sem.at[slot])
        return qp[block] + qcin[block].astype(F32)

    def q_along_y_sums(dzl):
        for dy in (2, 1, 3):
            slot = dzl * 4 + dy
            qst[slot] = core_sum(dy, dzl).astype(BF16)
            if dzl == 0:
                out.go(qst.at[slot], qyin.at[slot], qy_sem.at[slot], at.at_y(dy if dy < 3 else -1))
        if dzl == 1:
            for part, (first, count) in enumerate(PIECES):
                for dy in (2, 1, 3):
                    block = (4 + dy, pl.ds(first, count))
                    sem = qy_sem.at[4 + 4 * part + dy]
                    out.go(qst.at[block], qyin.at[block], sem, at.at_y(dy if dy < 3 else -1))

    def k_sum(dz):
        got(kx1.at[dz], kx1_sem.at[dz])
        got(kx1.at[4 + dz], kx1_sem.at[4 + dz])
        return kp[dz] + kx1[dz].astype(F32) + kx1[4 + dz].astype(F32)

    def k_send_z(dz, total):
        kst[pl.ds(krow(0, dz), ROWS)] = total.astype(BF16)
        send_k(0, dz, kzin.at[dz], kzin_sem.at[dz], at.at_zh(dz if dz < 3 else -1))

    for part, (first, count) in enumerate(PIECES):
        rows = pl.ds(first, count)
        got(kx2.at[1, rows], kx2_sem.at[1 + part])
        got(kx1.at[2, rows], kx1_sem.at[2 + 6 * part])
        got(kx1.at[6, rows], kx1_sem.at[6 + 3 * part])
        total = kp[2, rows] + kx1[2, rows].astype(F32) + kx1[6, rows].astype(F32)
        block = pl.ds(krow(0, 2) + first, count)
        kst[block] = (total + kx2[1, rows].astype(F32)).astype(BF16)
        out.go(kst.at[block], kzin.at[2, rows], kzin_sem.at[2 + 2 * part], at.at_zh(2))
    q_along_y_sums(1)
    k_send_z(3, k_sum(3))
    q_along_y_sums(0)
    k_send_z(1, k_sum(1))
    for side in (0, 1):
        got(kzt.at[side], kzt_sem.at[side])
    kst[pl.ds(krow(2, 0), ROWS)] = (kp[4] + kzt[0].astype(F32) + kzt[1].astype(F32)).astype(BF16)
    send_k(2, 0, kx2.at[0], kx2_sem.at[0], at.at_x(2))

    own = core_sum(0, 1)
    for part, (first, count) in enumerate(PIECES):
        rows = pl.ds(first, count)
        total = own[first : first + count]
        for dy in (1, 3, 2):
            got(qyin.at[4 + dy, rows], qy_sem.at[4 + 4 * part + dy])
            total = total + qyin[4 + dy, rows].astype(F32)
        qzst[rows] = total.astype(BF16)
        out.go(qzst.at[rows], qzin.at[rows], qz_sem.at[part], at.at_zl())
    q_total = core_sum(0, 0)
    for dy in (1, 3, 2):
        got(qyin.at[dy], qy_sem.at[dy])
        q_total = q_total + qyin[dy].astype(F32)
    total = k_sum(0)
    got(kx2.at[0], kx2_sem.at[0])
    total = total + kx2[0].astype(F32)
    for part, (first, count) in enumerate(PIECES):
        got(qzin.at[pl.ds(first, count)], qz_sem.at[part])
    both[0] = q_total + qzin[...].astype(F32)
    for dz in (1, 3, 2):
        if dz == 2:
            for part, (first, count) in enumerate(PIECES):
                got(kzin.at[2, pl.ds(first, count)], kzin_sem.at[2 + 2 * part])
        else:
            got(kzin.at[dz], kzin_sem.at[dz])
        total = total + kzin[dz].astype(F32)
    both[1] = total
    out.finish()


def local(queries, keys):
    frames = queries.shape[0] * lax.axis_size("row")
    scale = queries.shape[2] ** -0.5
    vmem = pl.BlockSpec(memory_space=pltpu.VMEM)
    hbm = pl.BlockSpec(memory_space=pltpu.MemorySpace.HBM)
    own = jax.ShapeDtypeStruct((1, ROWS, TOK), F32)

    def buf(*lead, dtype=BF16):
        return pltpu.VMEM((*lead, TOK), dtype)

    def sems(count):
        return pltpu.SemaphoreType.DMA((count,))

    both = pl.pallas_call(
        functools.partial(cycle_kernel, scale, frames),
        out_shape=jax.ShapeDtypeStruct((2, ROWS, TOK), F32),
        in_specs=[hbm, hbm],
        out_specs=vmem,
        scratch_shapes=[
            buf(TOK), buf(TOK),
            *pair_scratch(),
            buf(TOK), buf(5, ROWS, dtype=F32), buf(8, ROWS), buf(2, ROWS), buf(2, ROWS), buf(4, ROWS),
            buf(8 * ROWS), buf(8 * ROWS), buf(8 * ROWS, dtype=F32), buf(8, ROWS), buf(8, ROWS), buf(ROWS), buf(ROWS),
            sems(2), sems(68), sems(16), sems(16),
            sems(10), sems(3), sems(2), sems(5), sems(8), sems(12), sems(2),
        ],
        compiler_params=pltpu.CompilerParams(
            collective_id=0, has_side_effects=True, vmem_limit_bytes=44 * 2**20
        ),
        name="cycle_pairs",
    )(
        pltpu.with_memory_space_constraint(queries, pltpu.HBM),
        pltpu.with_memory_space_constraint(keys, pltpu.HBM),
    )
    return (both[0:1], both[1:2])


def solution(mesh):
    placed = (P("row", "col", None), P("col", "row", None))
    return jax.shard_map(
        local,
        mesh=mesh,
        in_specs=placed,
        out_specs=(P("row", "col", None), P("col", "row", None)),
        check_vma=False,
    )
```

```python
import functools
import math

import jax
import jax.numpy as jnp
from jax import lax
from jax.experimental import pallas as pl
from jax.experimental.pallas import tpu as pltpu
from jax.sharding import PartitionSpec as P

MESH = pl.DeviceIdType.MESH
BF16 = jnp.bfloat16
F32 = jnp.float32


class Place:
    def __init__(self):
        row = lax.axis_index("row")
        col = lax.axis_index("col")
        self.zh, self.x = row // 4, row % 4
        self.y, self.zl, self.c = col // 4, (col // 2) % 2, col % 2
        self.row, self.col = row, col

    def at_x(self, step):
        return (self.zh * 4 + (self.x + step + 4) % 4, self.col)

    def at_zh(self, step):
        return (((self.zh + step + 4) % 4) * 4 + self.x, self.col)

    def at_y(self, step):
        return (self.row, ((self.y + step + 4) % 4) * 4 + self.zl * 2 + self.c)

    def at_zl(self):
        return (self.row, self.y * 4 + (1 - self.zl) * 2 + self.c)

    def at_core(self):
        return (self.row, self.y * 4 + self.zl * 2 + 1 - self.c)


def greet(at):
    barrier = pltpu.get_barrier_semaphore()
    others = [at.at_core(), at.at_zl()]
    for step in (1, -1, 2):
        others += [at.at_x(step), at.at_y(step), at.at_zh(step)]
    for other in others:
        pl.semaphore_signal(barrier, inc=1, device_id=other, device_id_type=MESH)
    pl.semaphore_wait(barrier, len(others))


class Sends:
    def __init__(self, send_sem):
        self.send_sem = send_sem
        self.started = []

    def go(self, src, dst, recv, device):
        copy = pltpu.make_async_remote_copy(
            src_ref=src,
            dst_ref=dst,
            send_sem=self.send_sem.at[len(self.started)],
            recv_sem=recv,
            device_id=device,
            device_id_type=MESH,
        )
        copy.start()
        self.started.append(copy)

    def finish(self):
        for copy in self.started:
            copy.wait_send()


TOK = 768
ROWS = 48
KC = 192


def nt(a, b):
    return lax.dot_general(a, b, (((1,), (1,)), ((), ())), preferred_element_type=F32)


def nn(a, b):
    return lax.dot_general(a, b, (((1,), (0,)), ((), ())), preferred_element_type=F32)


def tn(a, b):
    return lax.dot_general(a, b, (((0,), (0,)), ((), ())), preferred_element_type=F32)


def fold(x, op):
    return op(x.reshape(x.shape[0] // 8, 8, x.shape[1]), axis=0)


class Pair:
    def __init__(self, scale, frames, qf, kf, st, bt, at, bh, ah, v, gr, gh, dv, ds, cmax, etop, csum, cdel):
        self.__dict__.update(locals())

    def scores(self, start, size):
        rows = pl.ds(start, size)
        st = nt(self.kf[rows], self.qf[...]) * (self.scale * math.log2(math.e))
        self.st[rows] = st
        top = fold(st, jnp.max)
        self.cmax[...] = top if start == 0 else jnp.maximum(self.cmax[...], top)
        e = jnp.exp2(st - jnp.max(st, axis=1, keepdims=True))
        b = e * (1.0 / jnp.sum(e, axis=1, keepdims=True))
        self.bt[rows] = b
        bh = b.astype(BF16)
        self.bh[rows] = bh
        self.v[rows] = nn(bh, self.qf[...]).astype(BF16)

    def powers(self, start, size, top):
        total = jnp.zeros((8, TOK), F32)
        for first in range(start, start + size, KC):
            rows = pl.ds(first, KC)
            e = jnp.exp2(self.st[rows] - top)
            self.at[rows] = e
            total = total + fold(e, jnp.sum)
        return total

    def attend_early(self, size):
        top = jnp.max(self.cmax[...], axis=0, keepdims=True)
        self.etop[...] = jnp.broadcast_to(top, (8, TOK))
        self.csum[...] = self.powers(0, size, top)

    def attend(self, size):
        top = jnp.max(self.cmax[...], axis=0, keepdims=True)
        early = jnp.exp2(self.etop[0:1] - top)
        late = self.powers(size, TOK - size, top)
        total = jnp.sum(self.csum[...] * early + late, axis=0, keepdims=True)
        inv = 1.0 / total
        weight = early * inv
        halves = jnp.zeros((8, TOK), F32)
        for first in range(0, TOK, KC):
            rows = pl.ds(first, KC)
            a = self.at[rows] * (weight if first < size else inv)
            self.at[rows] = a
            ah = a.astype(BF16)
            self.ah[rows] = ah
            halves = halves + fold(ah.astype(F32), jnp.sum)
        self.csum[...] = jnp.broadcast_to(jnp.sum(halves, axis=0, keepdims=True), (8, TOK))

    def residual(self, size=384):
        for c in range(TOK // size):
            rows = pl.ds(c * size, size)
            cycled = tn(self.ah[:, rows], self.v[...])
            g = (cycled - self.qf[rows].astype(F32)) * (1.0 / self.frames)
            gh = g.astype(BF16)
            self.gr[rows] = g
            self.gh[rows] = gh
            delta = jnp.sum(gh.astype(F32) * cycled, axis=1, keepdims=True)
            self.cdel[:, rows] = jnp.broadcast_to(delta, (size, 128)).T[0:8] / self.csum[:, rows]

    def grad_scores(self, start, size):
        rows = pl.ds(start, size)
        da = nt(self.v[rows], self.gh[...])
        dv = nn(self.ah[rows], self.gh[...]).astype(BF16)
        self.dv[rows] = dv
        db = nt(dv, self.qf[...])
        b = self.bt[rows]
        delta = jnp.sum(db * b, axis=1, keepdims=True)
        ds = self.at[rows] * (da - self.cdel[0:1]) + b * (db - delta)
        self.ds[rows] = (ds * self.scale).astype(BF16)

    def key_terms(self, c, size=KC):
        return nn(self.ds[pl.ds(c * size, size)], self.qf[...])

    def query_terms(self, c, size=384):
        rows = pl.ds(c * size, size)
        return tn(self.bh[:, rows], self.dv[...]) + tn(self.ds[:, rows], self.kf[...]) - self.gr[rows]


def pair_scratch():
    def whole(dtype):
        return pltpu.VMEM((TOK, TOK), dtype)

    return [
        whole(F32), whole(F32), whole(F32), whole(BF16), whole(BF16), whole(BF16),
        whole(F32), whole(BF16), whole(BF16), whole(BF16),
        *[pltpu.VMEM((8, TOK), F32)] * 4,
    ]


ZORDER = (0, 1, 3, 2)


PIECES = ((0, 32), (32, 16))


def krow(dx, dz):
    return (ZORDER.index(dz % 4) * 4 + dx % 4) * ROWS


def qrow(dy, dzl, dc):
    return (((1 - dzl) * 2 + 1 - dc) * 4 + dy % 4) * ROWS


def cycle_kernel(scale, frames, q_hbm, k_hbm, both, qf, kf, *scratch):
    pair = Pair(scale, frames, qf, kf, *scratch[:14])
    (
        kst, kp, kx1, kx2, kzt, kzin, qcst, qcin, qp, qst, qyin, qzst, qzin,
        own_sem, send_sem, q_sem, k_sem,
        kx1_sem, kx2_sem, kzt_sem, kzin_sem, qc_sem, qy_sem, qz_sem,
    ) = scratch[14:]
    at = Place()

    def kblock(dx, dz):
        return kf.at[pl.ds(krow(dx, dz), ROWS)]

    def qblock(dy, dzl, dc):
        return qf.at[pl.ds(qrow(dy, dzl, dc), ROWS)]

    own_q = pltpu.make_async_copy(q_hbm.at[0], qblock(0, 0, 0), own_sem.at[0])
    own_k = pltpu.make_async_copy(k_hbm.at[0], kblock(0, 0), own_sem.at[1])
    own_q.start()
    own_k.start()
    greet(at)
    own_q.wait()
    own_k.wait()
    out = Sends(send_sem)

    def got(ref, sem):
        pltpu.make_async_remote_copy(
            src_ref=ref, dst_ref=ref, send_sem=send_sem.at[0],
            recv_sem=sem, device_id=at.at_core(), device_id_type=MESH,
        ).wait_recv()


    def ksem(dx, dz):
        return k_sem.at[krow(dx, dz) // ROWS]

    def qsem(dy, dzl, dc):
        return q_sem.at[qrow(dy, dzl, dc) // ROWS]

    def got_k(dx, dz):
        got(kblock(dx, dz), ksem(dx, dz))

    def got_q(dy, dzl, dc):
        got(qblock(dy, dzl, dc), qsem(dy, dzl, dc))

    def k_along_x(dz, steps):
        for step in steps:
            out.go(kblock(0, dz), kblock(-step, dz), ksem(-step, dz), at.at_x(step))

    def far_piece(dx, part):
        first, count = PIECES[part]
        return kf.at[pl.ds(krow(dx, 2) + first, count)]

    def far_sem(dx, part):
        return k_sem.at[krow(dx, 2) // ROWS + 4 * part]

    def k_along_z(dx, steps):
        for step in steps:
            out.go(kblock(dx, 0), kblock(dx, -step), ksem(dx, -step), at.at_zh(step))

    def q_along_y(dzl):
        for step in (1, -1, 2):
            out.go(qblock(0, dzl, 0), qblock(-step, dzl, 0), qsem(-step, dzl, 0), at.at_y(step))

    def q_to_core(dy, dzl):
        out.go(qblock(dy, dzl, 0), qblock(dy, dzl, 1), qsem(dy, dzl, 1), at.at_core())

    out.go(qblock(0, 0, 0), qblock(0, 1, 0), qsem(0, 1, 0), at.at_zl())
    k_along_z(0, (1, -1))
    k_along_x(0, (2, 1, -1))
    q_along_y(0)
    for part, (first, count) in enumerate(PIECES):
        src = kf.at[pl.ds(krow(0, 0) + first, count)]
        out.go(src, far_piece(0, part), far_sem(0, part), at.at_zh(2))
    q_to_core(0, 0)

    got_q(0, 1, 0)
    q_along_y(1)
    q_to_core(0, 1)
    for dy in (1, 3):
        got_q(dy, 0, 0)
        q_to_core(dy, 0)
    got_k(2, 0)
    k_along_z(2, (1, -1))
    got_q(2, 0, 0)
    q_to_core(2, 0)
    for dz in (1, 3):
        got_k(0, dz)
        k_along_x(dz, (1, -1))
    for dy in (1, 3, 2):
        got_q(dy, 1, 0)
        q_to_core(dy, 1)
    for part in (0, 1):
        got(far_piece(0, part), far_sem(0, part))
        for step in (2, 1, -1):
            dx = -step % 4
            out.go(far_piece(0, part), far_piece(dx, part), far_sem(dx, part), at.at_x(step))
    for dzl in (0, 1):
        for dy in (0, 1, 3, 2):
            got_q(dy, dzl, 1)

    got_k(1, 0)
    got_k(3, 0)
    pair.scores(0, KC)
    for dz in (1, 3):
        for dx in (1, 3, 2):
            got_k(dx, dz)
    pair.scores(KC, 2 * KC)
    pair.attend_early(3 * KC)
    for dx in (1, 3, 2):
        for part in (0, 1):
            got(far_piece(dx, part), far_sem(dx, part))
    pair.scores(3 * KC, KC)
    pair.attend(3 * KC)
    pair.residual()

    def send_k(dx, dz, dst, sem, device):
        out.go(kst.at[pl.ds(krow(dx, dz), ROWS)], dst, sem, device)

    def key_terms(dz):
        c = ZORDER.index(dz)
        terms = pair.key_terms(c)
        kst[pl.ds(c * KC, KC)] = terms.astype(BF16)
        kp[dz] = terms[0:ROWS]
        if dz == 0:
            kp[4] = terms[2 * ROWS : 3 * ROWS]
        if dz == 1:
            send_k(2, 1, kzt.at[0], kzt_sem.at[0], at.at_zh(1))
        if dz == 3:
            send_k(2, 3, kzt.at[1], kzt_sem.at[1], at.at_zh(-1))
        if dz == 2:
            for part, (first, count) in enumerate(PIECES):
                rows = pl.ds(first, count)
                for dx, dst, sem, device in (
                    (2, kx2.at[1, rows], kx2_sem.at[1 + part], at.at_x(2)),
                    (1, kx1.at[2, rows], kx1_sem.at[2 + 6 * part], at.at_x(1)),
                    (3, kx1.at[6, rows], kx1_sem.at[6 + 3 * part], at.at_x(-1)),
                ):
                    out.go(kst.at[pl.ds(krow(dx, 2) + first, count)], dst, sem, device)
            return
        send_k(1, dz, kx1.at[dz], kx1_sem.at[dz], at.at_x(1))
        send_k(3, dz, kx1.at[4 + dz], kx1_sem.at[4 + dz], at.at_x(-1))

    def query_terms(dzl):
        terms = pair.query_terms(1 - dzl)
        rows = pl.ds(dzl * KC, KC)
        qcst[rows] = terms[0:KC].astype(BF16)
        qp[rows] = terms[KC : 2 * KC]
        for dy in (2, 1, 3, 0):
            slot = dzl * 4 + dy
            block = pl.ds(slot * ROWS, ROWS)
            out.go(qcst.at[block], qcin.at[block], qc_sem.at[slot], at.at_core())

    pair.grad_scores(3 * KC, KC)
    key_terms(2)
    pair.grad_scores(0, 3 * KC)
    key_terms(1)
    key_terms(3)
    query_terms(1)
    key_terms(0)
    query_terms(0)

    def core_sum(dy, dzl):
        slot = dzl * 4 + dy
        block = pl.ds(slot * ROWS, ROWS)
        got(qcin.at[block], qc_sem.at[slot])
        return qp[block] + qcin[block].astype(F32)

    def q_along_y_sums(dzl):
        for dy in (2, 1, 3):
            slot = dzl * 4 + dy
            qst[slot] = core_sum(dy, dzl).astype(BF16)
            if dzl == 0:
                out.go(qst.at[slot], qyin.at[slot], qy_sem.at[slot], at.at_y(dy if dy < 3 else -1))
        if dzl == 1:
            for part, (first, count) in enumerate(PIECES):
                for dy in (2, 1, 3):
                    block = (4 + dy, pl.ds(first, count))
                    sem = qy_sem.at[4 + 4 * part + dy]
                    out.go(qst.at[block], qyin.at[block], sem, at.at_y(dy if dy < 3 else -1))

    def k_sum(dz):
        got(kx1.at[dz], kx1_sem.at[dz])
        got(kx1.at[4 + dz], kx1_sem.at[4 + dz])
        return kp[dz] + kx1[dz].astype(F32) + kx1[4 + dz].astype(F32)

    def k_send_z(dz, total):
        kst[pl.ds(krow(0, dz), ROWS)] = total.astype(BF16)
        send_k(0, dz, kzin.at[dz], kzin_sem.at[dz], at.at_zh(dz if dz < 3 else -1))

    for part, (first, count) in enumerate(PIECES):
        rows = pl.ds(first, count)
        got(kx2.at[1, rows], kx2_sem.at[1 + part])
        got(kx1.at[2, rows], kx1_sem.at[2 + 6 * part])
        got(kx1.at[6, rows], kx1_sem.at[6 + 3 * part])
        total = kp[2, rows] + kx1[2, rows].astype(F32) + kx1[6, rows].astype(F32)
        block = pl.ds(krow(0, 2) + first, count)
        kst[block] = (total + kx2[1, rows].astype(F32)).astype(BF16)
        out.go(kst.at[block], kzin.at[2, rows], kzin_sem.at[2 + 2 * part], at.at_zh(2))
    q_along_y_sums(1)
    k_send_z(3, k_sum(3))
    q_along_y_sums(0)
    k_send_z(1, k_sum(1))
    for side in (0, 1):
        got(kzt.at[side], kzt_sem.at[side])
    kst[pl.ds(krow(2, 0), ROWS)] = (kp[4] + kzt[0].astype(F32) + kzt[1].astype(F32)).astype(BF16)
    send_k(2, 0, kx2.at[0], kx2_sem.at[0], at.at_x(2))

    own = core_sum(0, 1)
    for part, (first, count) in enumerate(PIECES):
        rows = pl.ds(first, count)
        total = own[first : first + count]
        for dy in (1, 3, 2):
            got(qyin.at[4 + dy, rows], qy_sem.at[4 + 4 * part + dy])
            total = total + qyin[4 + dy, rows].astype(F32)
        qzst[rows] = total.astype(BF16)
        out.go(qzst.at[rows], qzin.at[rows], qz_sem.at[part], at.at_zl())
    q_total = core_sum(0, 0)
    for dy in (1, 3, 2):
        got(qyin.at[dy], qy_sem.at[dy])
        q_total = q_total + qyin[dy].astype(F32)
    total = k_sum(0)
    got(kx2.at[0], kx2_sem.at[0])
    total = total + kx2[0].astype(F32)
    for part, (first, count) in enumerate(PIECES):
        got(qzin.at[pl.ds(first, count)], qz_sem.at[part])
    both[0] = q_total + qzin[...].astype(F32)
    for dz in (1, 3, 2):
        if dz == 2:
            for part, (first, count) in enumerate(PIECES):
                got(kzin.at[2, pl.ds(first, count)], kzin_sem.at[2 + 2 * part])
        else:
            got(kzin.at[dz], kzin_sem.at[dz])
        total = total + kzin[dz].astype(F32)
    both[1] = total
    out.finish()


def local(queries, keys):
    frames = queries.shape[0] * lax.axis_size("row")
    scale = queries.shape[2] ** -0.5
    vmem = pl.BlockSpec(memory_space=pltpu.VMEM)
    hbm = pl.BlockSpec(memory_space=pltpu.MemorySpace.HBM)
    own = jax.ShapeDtypeStruct((1, ROWS, TOK), F32)

    def buf(*lead, dtype=BF16):
        return pltpu.VMEM((*lead, TOK), dtype)

    def sems(count):
        return pltpu.SemaphoreType.DMA((count,))

    both = pl.pallas_call(
        functools.partial(cycle_kernel, scale, frames),
        out_shape=jax.ShapeDtypeStruct((2, ROWS, TOK), F32),
        in_specs=[hbm, hbm],
        out_specs=vmem,
        scratch_shapes=[
            buf(TOK), buf(TOK),
            *pair_scratch(),
            buf(TOK), buf(5, ROWS, dtype=F32), buf(8, ROWS), buf(2, ROWS), buf(2, ROWS), buf(4, ROWS),
            buf(8 * ROWS), buf(8 * ROWS), buf(8 * ROWS, dtype=F32), buf(8, ROWS), buf(8, ROWS), buf(ROWS), buf(ROWS),
            sems(2), sems(72), sems(16), sems(20),
            sems(10), sems(3), sems(2), sems(5), sems(8), sems(12), sems(2),
        ],
        compiler_params=pltpu.CompilerParams(
            collective_id=0, has_side_effects=True, vmem_limit_bytes=44 * 2**20
        ),
        name="cycle_pairs",
    )(
        pltpu.with_memory_space_constraint(queries, pltpu.HBM),
        pltpu.with_memory_space_constraint(keys, pltpu.HBM),
    )
    return (both[0:1], both[1:2])


def solution(mesh):
    placed = (P("row", "col", None), P("col", "row", None))
    return jax.shard_map(
        local,
        mesh=mesh,
        in_specs=placed,
        out_specs=(P("row", "col", None), P("col", "row", None)),
        check_vma=False,
    )
```

```python
import functools
import math

import jax
import jax.numpy as jnp
from jax import lax
from jax.experimental import pallas as pl
from jax.experimental.pallas import tpu as pltpu
from jax.sharding import PartitionSpec as P

MESH = pl.DeviceIdType.MESH
BF16 = jnp.bfloat16
F32 = jnp.float32


class Place:
    def __init__(self):
        row = lax.axis_index("row")
        col = lax.axis_index("col")
        self.zh, self.x = row // 4, row % 4
        self.y, self.zl, self.c = col // 4, (col // 2) % 2, col % 2
        self.row, self.col = row, col

    def at_x(self, step):
        return (self.zh * 4 + (self.x + step + 4) % 4, self.col)

    def at_zh(self, step):
        return (((self.zh + step + 4) % 4) * 4 + self.x, self.col)

    def at_y(self, step):
        return (self.row, ((self.y + step + 4) % 4) * 4 + self.zl * 2 + self.c)

    def at_zl(self):
        return (self.row, self.y * 4 + (1 - self.zl) * 2 + self.c)

    def at_core(self):
        return (self.row, self.y * 4 + self.zl * 2 + 1 - self.c)


def greet(at):
    barrier = pltpu.get_barrier_semaphore()
    others = [at.at_core(), at.at_zl()]
    for step in (1, -1, 2):
        others += [at.at_x(step), at.at_y(step), at.at_zh(step)]
    for other in others:
        pl.semaphore_signal(barrier, inc=1, device_id=other, device_id_type=MESH)
    pl.semaphore_wait(barrier, len(others))


class Sends:
    def __init__(self, send_sem):
        self.send_sem = send_sem
        self.started = []

    def go(self, src, dst, recv, device):
        copy = pltpu.make_async_remote_copy(
            src_ref=src,
            dst_ref=dst,
            send_sem=self.send_sem.at[len(self.started)],
            recv_sem=recv,
            device_id=device,
            device_id_type=MESH,
        )
        copy.start()
        self.started.append(copy)

    def finish(self):
        for copy in self.started:
            copy.wait_send()


TOK = 768
ROWS = 48
KC = 192


def nt(a, b):
    return lax.dot_general(a, b, (((1,), (1,)), ((), ())), preferred_element_type=F32)


def nn(a, b):
    return lax.dot_general(a, b, (((1,), (0,)), ((), ())), preferred_element_type=F32)


def tn(a, b):
    return lax.dot_general(a, b, (((0,), (0,)), ((), ())), preferred_element_type=F32)


def fold(x, op):
    return op(x.reshape(x.shape[0] // 8, 8, x.shape[1]), axis=0)


class Pair:
    def __init__(self, scale, frames, qf, kf, st, bt, at, bh, ah, v, gr, gh, dv, ds, cmax, etop, csum, cdel):
        self.__dict__.update(locals())

    def scores(self, start, size):
        rows = pl.ds(start, size)
        st = nt(self.kf[rows], self.qf[...]) * (self.scale * math.log2(math.e))
        self.st[rows] = st
        top = fold(st, jnp.max)
        self.cmax[...] = top if start == 0 else jnp.maximum(self.cmax[...], top)
        e = jnp.exp2(st - jnp.max(st, axis=1, keepdims=True))
        b = e * (1.0 / jnp.sum(e, axis=1, keepdims=True))
        self.bt[rows] = b
        bh = b.astype(BF16)
        self.bh[rows] = bh
        self.v[rows] = nn(bh, self.qf[...]).astype(BF16)

    def powers(self, start, size, top):
        total = jnp.zeros((8, TOK), F32)
        for first in range(start, start + size, KC):
            rows = pl.ds(first, KC)
            e = jnp.exp2(self.st[rows] - top)
            self.at[rows] = e
            total = total + fold(e, jnp.sum)
        return total

    def attend_early(self, size):
        top = jnp.max(self.cmax[...], axis=0, keepdims=True)
        self.etop[...] = jnp.broadcast_to(top, (8, TOK))
        self.csum[...] = self.powers(0, size, top)

    def attend(self, size):
        top = jnp.max(self.cmax[...], axis=0, keepdims=True)
        early = jnp.exp2(self.etop[0:1] - top)
        late = self.powers(size, TOK - size, top)
        total = jnp.sum(self.csum[...] * early + late, axis=0, keepdims=True)
        inv = 1.0 / total
        weight = early * inv
        halves = jnp.zeros((8, TOK), F32)
        for first in range(0, TOK, KC):
            rows = pl.ds(first, KC)
            a = self.at[rows] * (weight if first < size else inv)
            self.at[rows] = a
            ah = a.astype(BF16)
            self.ah[rows] = ah
            halves = halves + fold(ah.astype(F32), jnp.sum)
        self.csum[...] = jnp.broadcast_to(jnp.sum(halves, axis=0, keepdims=True), (8, TOK))

    def residual(self, size=384):
        for c in range(TOK // size):
            rows = pl.ds(c * size, size)
            cycled = tn(self.ah[:, rows], self.v[...])
            g = (cycled - self.qf[rows].astype(F32)) * (1.0 / self.frames)
            gh = g.astype(BF16)
            self.gr[rows] = g
            self.gh[rows] = gh
            delta = jnp.sum(gh.astype(F32) * cycled, axis=1, keepdims=True)
            self.cdel[:, rows] = jnp.broadcast_to(delta, (size, 128)).T[0:8] / self.csum[:, rows]

    def grad_scores(self, start, size):
        rows = pl.ds(start, size)
        da = nt(self.v[rows], self.gh[...])
        dv = nn(self.ah[rows], self.gh[...]).astype(BF16)
        self.dv[rows] = dv
        db = nt(dv, self.qf[...])
        b = self.bt[rows]
        delta = jnp.sum(db * b, axis=1, keepdims=True)
        ds = self.at[rows] * (da - self.cdel[0:1]) + b * (db - delta)
        self.ds[rows] = (ds * self.scale).astype(BF16)

    def key_terms(self, c, size=KC):
        return nn(self.ds[pl.ds(c * size, size)], self.qf[...])

    def query_terms(self, c, size=384):
        rows = pl.ds(c * size, size)
        return tn(self.bh[:, rows], self.dv[...]) + tn(self.ds[:, rows], self.kf[...]) - self.gr[rows]


def pair_scratch():
    def whole(dtype):
        return pltpu.VMEM((TOK, TOK), dtype)

    return [
        whole(F32), whole(F32), whole(F32), whole(BF16), whole(BF16), whole(BF16),
        whole(F32), whole(BF16), whole(BF16), whole(BF16),
        *[pltpu.VMEM((8, TOK), F32)] * 4,
    ]


ZORDER = (0, 1, 3, 2)


PIECES = ((0, 32), (32, 16))


def krow(dx, dz):
    return (ZORDER.index(dz % 4) * 4 + dx % 4) * ROWS


def qrow(dy, dzl, dc):
    return (((1 - dzl) * 2 + 1 - dc) * 4 + dy % 4) * ROWS


def cycle_kernel(scale, frames, q_hbm, k_hbm, both, qf, kf, *scratch):
    pair = Pair(scale, frames, qf, kf, *scratch[:14])
    (
        kst, kp, kx1, kx2, kzt, kzin, qcst, qcin, qp, qst, qyin, qzst, qzin,
        own_sem, send_sem, q_sem, k_sem,
        kx1_sem, kx2_sem, kzt_sem, kzin_sem, qc_sem, qy_sem, qz_sem,
    ) = scratch[14:]
    at = Place()

    def kblock(dx, dz):
        return kf.at[pl.ds(krow(dx, dz), ROWS)]

    def qblock(dy, dzl, dc):
        return qf.at[pl.ds(qrow(dy, dzl, dc), ROWS)]

    own_q = pltpu.make_async_copy(q_hbm.at[0], qblock(0, 0, 0), own_sem.at[0])
    own_k = pltpu.make_async_copy(k_hbm.at[0], kblock(0, 0), own_sem.at[1])
    own_q.start()
    own_k.start()
    greet(at)
    own_q.wait()
    own_k.wait()
    out = Sends(send_sem)

    def got(ref, sem):
        pltpu.make_async_remote_copy(
            src_ref=ref, dst_ref=ref, send_sem=send_sem.at[0],
            recv_sem=sem, device_id=at.at_core(), device_id_type=MESH,
        ).wait_recv()


    def ksem(dx, dz):
        return k_sem.at[krow(dx, dz) // ROWS]

    def qsem(dy, dzl, dc):
        return q_sem.at[qrow(dy, dzl, dc) // ROWS]

    def got_k(dx, dz):
        got(kblock(dx, dz), ksem(dx, dz))

    def got_q(dy, dzl, dc):
        got(qblock(dy, dzl, dc), qsem(dy, dzl, dc))

    def k_along_x(dz, steps):
        for step in steps:
            out.go(kblock(0, dz), kblock(-step, dz), ksem(-step, dz), at.at_x(step))

    def far_piece(dx, part):
        first, count = PIECES[part]
        return kf.at[pl.ds(krow(dx, 2) + first, count)]

    def far_sem(dx, part):
        return k_sem.at[krow(dx, 2) // ROWS + 4 * part]

    def k_along_z(dx, steps):
        for step in steps:
            out.go(kblock(dx, 0), kblock(dx, -step), ksem(dx, -step), at.at_zh(step))

    def q_along_y(dzl):
        for step in (1, -1, 2):
            out.go(qblock(0, dzl, 0), qblock(-step, dzl, 0), qsem(-step, dzl, 0), at.at_y(step))

    def q_to_core(dy, dzl):
        out.go(qblock(dy, dzl, 0), qblock(dy, dzl, 1), qsem(dy, dzl, 1), at.at_core())

    out.go(qblock(0, 0, 0), qblock(0, 1, 0), qsem(0, 1, 0), at.at_zl())
    k_along_z(0, (1, -1))
    k_along_x(0, (1, -1, 2))
    q_along_y(0)
    for part, (first, count) in enumerate(PIECES):
        src = kf.at[pl.ds(krow(0, 0) + first, count)]
        out.go(src, far_piece(0, part), far_sem(0, part), at.at_zh(2))
    q_to_core(0, 0)

    got_q(0, 1, 0)
    q_along_y(1)
    q_to_core(0, 1)
    for dy in (1, 3):
        got_q(dy, 0, 0)
        q_to_core(dy, 0)
    got_k(2, 0)
    k_along_z(2, (1, -1))
    got_q(2, 0, 0)
    q_to_core(2, 0)
    for dz in (1, 3):
        got_k(0, dz)
        k_along_x(dz, (1, -1))
    for dy in (1, 3, 2):
        got_q(dy, 1, 0)
        q_to_core(dy, 1)
    for part in (0, 1):
        got(far_piece(0, part), far_sem(0, part))
        for step in (2, 1, -1):
            dx = -step % 4
            out.go(far_piece(0, part), far_piece(dx, part), far_sem(dx, part), at.at_x(step))
    for dzl in (0, 1):
        for dy in (0, 1, 3, 2):
            got_q(dy, dzl, 1)

    got_k(1, 0)
    got_k(3, 0)
    pair.scores(0, KC)
    for dz in (1, 3):
        for dx in (1, 3, 2):
            got_k(dx, dz)
    pair.scores(KC, 2 * KC)
    pair.attend_early(3 * KC)
    for dx in (1, 3, 2):
        for part in (0, 1):
            got(far_piece(dx, part), far_sem(dx, part))
    pair.scores(3 * KC, KC)
    pair.attend(3 * KC)
    pair.residual()

    def send_k(dx, dz, dst, sem, device):
        out.go(kst.at[pl.ds(krow(dx, dz), ROWS)], dst, sem, device)

    def key_terms(dz):
        c = ZORDER.index(dz)
        terms = pair.key_terms(c)
        kst[pl.ds(c * KC, KC)] = terms.astype(BF16)
        kp[dz] = terms[0:ROWS]
        if dz == 0:
            kp[4] = terms[2 * ROWS : 3 * ROWS]
        if dz == 1:
            send_k(2, 1, kzt.at[0], kzt_sem.at[0], at.at_zh(1))
        if dz == 3:
            send_k(2, 3, kzt.at[1], kzt_sem.at[1], at.at_zh(-1))
        if dz == 2:
            for part, (first, count) in enumerate(PIECES):
                rows = pl.ds(first, count)
                for dx, dst, sem, device in (
                    (2, kx2.at[1, rows], kx2_sem.at[1 + part], at.at_x(2)),
                    (1, kx1.at[2, rows], kx1_sem.at[2 + 6 * part], at.at_x(1)),
                    (3, kx1.at[6, rows], kx1_sem.at[6 + 3 * part], at.at_x(-1)),
                ):
                    out.go(kst.at[pl.ds(krow(dx, 2) + first, count)], dst, sem, device)
            return
        send_k(1, dz, kx1.at[dz], kx1_sem.at[dz], at.at_x(1))
        send_k(3, dz, kx1.at[4 + dz], kx1_sem.at[4 + dz], at.at_x(-1))

    def query_terms(dzl):
        terms = pair.query_terms(1 - dzl)
        rows = pl.ds(dzl * KC, KC)
        qcst[rows] = terms[0:KC].astype(BF16)
        qp[rows] = terms[KC : 2 * KC]
        for dy in (2, 1, 3, 0):
            slot = dzl * 4 + dy
            block = pl.ds(slot * ROWS, ROWS)
            out.go(qcst.at[block], qcin.at[block], qc_sem.at[slot], at.at_core())

    pair.grad_scores(3 * KC, KC)
    key_terms(2)
    pair.grad_scores(0, 3 * KC)
    key_terms(1)
    key_terms(3)
    query_terms(1)
    key_terms(0)
    query_terms(0)

    def core_sum(dy, dzl):
        slot = dzl * 4 + dy
        block = pl.ds(slot * ROWS, ROWS)
        got(qcin.at[block], qc_sem.at[slot])
        return qp[block] + qcin[block].astype(F32)

    def q_along_y_sums(dzl):
        for dy in (2, 1, 3):
            slot = dzl * 4 + dy
            qst[slot] = core_sum(dy, dzl).astype(BF16)
            if dzl == 0:
                out.go(qst.at[slot], qyin.at[slot], qy_sem.at[slot], at.at_y(dy if dy < 3 else -1))
        if dzl == 1:
            for part, (first, count) in enumerate(PIECES):
                for dy in (2, 1, 3):
                    block = (4 + dy, pl.ds(first, count))
                    sem = qy_sem.at[4 + 4 * part + dy]
                    out.go(qst.at[block], qyin.at[block], sem, at.at_y(dy if dy < 3 else -1))

    def k_sum(dz):
        got(kx1.at[dz], kx1_sem.at[dz])
        got(kx1.at[4 + dz], kx1_sem.at[4 + dz])
        return kp[dz] + kx1[dz].astype(F32) + kx1[4 + dz].astype(F32)

    def k_send_z(dz, total):
        kst[pl.ds(krow(0, dz), ROWS)] = total.astype(BF16)
        send_k(0, dz, kzin.at[dz], kzin_sem.at[dz], at.at_zh(dz if dz < 3 else -1))

    for part, (first, count) in enumerate(PIECES):
        rows = pl.ds(first, count)
        got(kx2.at[1, rows], kx2_sem.at[1 + part])
        got(kx1.at[2, rows], kx1_sem.at[2 + 6 * part])
        got(kx1.at[6, rows], kx1_sem.at[6 + 3 * part])
        total = kp[2, rows] + kx1[2, rows].astype(F32) + kx1[6, rows].astype(F32)
        block = pl.ds(krow(0, 2) + first, count)
        kst[block] = (total + kx2[1, rows].astype(F32)).astype(BF16)
        out.go(kst.at[block], kzin.at[2, rows], kzin_sem.at[2 + 2 * part], at.at_zh(2))
    q_along_y_sums(1)
    k_send_z(3, k_sum(3))
    q_along_y_sums(0)
    k_send_z(1, k_sum(1))
    for side in (0, 1):
        got(kzt.at[side], kzt_sem.at[side])
    kst[pl.ds(krow(2, 0), ROWS)] = (kp[4] + kzt[0].astype(F32) + kzt[1].astype(F32)).astype(BF16)
    send_k(2, 0, kx2.at[0], kx2_sem.at[0], at.at_x(2))

    own = core_sum(0, 1)
    for part, (first, count) in enumerate(PIECES):
        rows = pl.ds(first, count)
        total = own[first : first + count]
        for dy in (1, 3, 2):
            got(qyin.at[4 + dy, rows], qy_sem.at[4 + 4 * part + dy])
            total = total + qyin[4 + dy, rows].astype(F32)
        qzst[rows] = total.astype(BF16)
        out.go(qzst.at[rows], qzin.at[rows], qz_sem.at[part], at.at_zl())
    q_total = core_sum(0, 0)
    for dy in (1, 3, 2):
        got(qyin.at[dy], qy_sem.at[dy])
        q_total = q_total + qyin[dy].astype(F32)
    total = k_sum(0)
    got(kx2.at[0], kx2_sem.at[0])
    total = total + kx2[0].astype(F32)
    for part, (first, count) in enumerate(PIECES):
        got(qzin.at[pl.ds(first, count)], qz_sem.at[part])
    both[0] = q_total + qzin[...].astype(F32)
    for dz in (1, 3, 2):
        if dz == 2:
            for part, (first, count) in enumerate(PIECES):
                got(kzin.at[2, pl.ds(first, count)], kzin_sem.at[2 + 2 * part])
        else:
            got(kzin.at[dz], kzin_sem.at[dz])
        total = total + kzin[dz].astype(F32)
    both[1] = total
    out.finish()


def local(queries, keys):
    frames = queries.shape[0] * lax.axis_size("row")
    scale = queries.shape[2] ** -0.5
    vmem = pl.BlockSpec(memory_space=pltpu.VMEM)
    hbm = pl.BlockSpec(memory_space=pltpu.MemorySpace.HBM)
    own = jax.ShapeDtypeStruct((1, ROWS, TOK), F32)

    def buf(*lead, dtype=BF16):
        return pltpu.VMEM((*lead, TOK), dtype)

    def sems(count):
        return pltpu.SemaphoreType.DMA((count,))

    both = pl.pallas_call(
        functools.partial(cycle_kernel, scale, frames),
        out_shape=jax.ShapeDtypeStruct((2, ROWS, TOK), F32),
        in_specs=[hbm, hbm],
        out_specs=vmem,
        scratch_shapes=[
            buf(TOK), buf(TOK),
            *pair_scratch(),
            buf(TOK), buf(5, ROWS, dtype=F32), buf(8, ROWS), buf(2, ROWS), buf(2, ROWS), buf(4, ROWS),
            buf(8 * ROWS), buf(8 * ROWS), buf(8 * ROWS, dtype=F32), buf(8, ROWS), buf(8, ROWS), buf(ROWS), buf(ROWS),
            sems(2), sems(72), sems(16), sems(20),
            sems(10), sems(3), sems(2), sems(5), sems(8), sems(12), sems(2),
        ],
        compiler_params=pltpu.CompilerParams(
            collective_id=0, has_side_effects=True, vmem_limit_bytes=44 * 2**20
        ),
        name="cycle_pairs",
    )(
        pltpu.with_memory_space_constraint(queries, pltpu.HBM),
        pltpu.with_memory_space_constraint(keys, pltpu.HBM),
    )
    return (both[0:1], both[1:2])


def solution(mesh):
    placed = (P("row", "col", None), P("col", "row", None))
    return jax.shard_map(
        local,
        mesh=mesh,
        in_specs=placed,
        out_specs=(P("row", "col", None), P("col", "row", None)),
        check_vma=False,
    )
```
